128 devices in a mesh: fsdp: 16 (over z, x_lo, core), tp: 8 (over x_hi, y).
Axes of the slice: x: 4 (x_hi: 2, x_lo: 2; x = x_hi * 2 + x_lo), y: 4, z: 4, core: 2. Of those that a mesh axis runs over, the one named last changes fastest.
Arguments:
- states: bfloat16 [512, 4, 8192], P('fsdp'), may hold values from -6 to 6
- norm_gain: float32 [8192], replicated, may hold values from 0.5 to 1.5
- query_base: bfloat16 [8192, 8192], P(('fsdp', 'tp')), may hold values from -0.0625 to 0.0625
- key_base: bfloat16 [8192, 1024], P(('fsdp', 'tp')), may hold values from -0.0625 to 0.0625
- value_base: bfloat16 [8192, 1024], P(('fsdp', 'tp')), may hold values from -0.0625 to 0.0625
- output_base: bfloat16 [8192, 8192], P(('fsdp', 'tp')), may hold values from -0.5 to 0.5
- query_down: bfloat16 [4, 8192, 64], P(None, ('fsdp', 'tp')), may hold values from -0.0625 to 0.0625
- query_up: bfloat16 [4, 64, 8192], replicated, may hold values from -0.75 to 0.75
- key_down: bfloat16 [4, 8192, 64], P(None, ('fsdp', 'tp')), may hold values from -0.0625 to 0.0625
- key_up: bfloat16 [4, 64, 1024], replicated, may hold values from -0.75 to 0.75
- value_down: bfloat16 [4, 8192, 64], P(None, ('fsdp', 'tp')), may hold values from -0.0625 to 0.0625
- value_up: bfloat16 [4, 64, 1024], replicated, may hold values from -0.75 to 0.75
- output_down: bfloat16 [4, 8192, 64], P(None, ('fsdp', 'tp')), may hold values from -0.5 to 0.5
- output_up: bfloat16 [4, 64, 8192], replicated, may hold values from -0.75 to 0.75
- adapter_layer: int32 [1], replicated, may hold values from 0 to 3
- kv_lengths: int32 [512], P('fsdp'), may hold values from 8 to 512
- cache_keys: bfloat16 [512, 512, 8, 128], P('fsdp', None, 'tp'), may hold values from -320 to 320
- cache_values: bfloat16 [512, 512, 8, 128], P('fsdp', None, 'tp'), may hold values from -6 to 6
Outputs:
- layer_update: bfloat16 [512, 4, 8192], P('fsdp', None, 'tp')
The draws below stay inside these ranges and needn't reach their ends.
Inputs may be any that keep to these rules, and one draw needn't show every extreme that they name: `kv_lengths`: slots at and beyond a sequence's length hold no cached position.
All inputs are finite; a program needn't handle non-finite values.
Results may differ from the reference program's by a relative error of at most 0.012.
The reference program's roundings to bfloat16 on the way count: a program that leaves them out, or rounds other values in their place, can miss the bound.
Values may be sent and summed in bfloat16 or wider, within the bound.
A program may use at most 128 MiB of HBM per device.

```python
import jax
import jax.numpy as jnp
from jax import lax

D = 8192
HQ = 64
KVH = 8
DH = 128
R = 64
SLOTS = 4
STEPS = 4
SEQ_DEV = 32
LEN = 512
SEQS = 512
N_FSDP = 16


def draw_cache_keys(key, part):
    array_shape = (SEQS, LEN, KVH, DH)
    standard = jnp.clip(jax.random.normal(jax.random.fold_in(key, 11), array_shape, jnp.float32), -4.0, 4.0)
    return standard.astype(jnp.bfloat16)


def plant(array, key, least, high):
    place = [jax.random.randint(jax.random.fold_in(key, axis), (), 0, length) for axis, length in enumerate(array.shape)]
    longest = array.shape.index(max(array.shape))
    beside = place[:longest] + [(place[longest] + 1) % array.shape[longest]] + place[longest + 1:]
    return array.at[tuple(place)].set(least).at[tuple(beside)].set(high)


def steps_of(rng, extent, cuts, least, high):
    gain = 1.0
    for dim, parts in cuts:
        heights = jax.random.uniform(jax.random.fold_in(jax.random.fold_in(rng, 6), dim), (parts,), jnp.float32, least / len(cuts), high / len(cuts))
        gain = gain * jnp.repeat(jnp.exp(heights), extent[dim] // parts).reshape((-1,) + (1,) * (len(extent) - 1 - dim))
    return gain


def scatter_about(rng, extent, scale, limit, cuts=(), kind=jnp.bfloat16):
    factor_of = steps_of(rng, extent, cuts, -0.22, 0.18) if cuts else 1.0
    result = jax.random.normal(rng, extent, jnp.float32) * scale * factor_of
    return jnp.minimum(jnp.maximum(result, -limit), limit).astype(kind)


def setup_inputs(seed: int = 0) -> dict:
    streams_of = jax.random.split(jax.random.key(seed), 19)
    states = scatter_about(streams_of[0], (SEQS, STEPS, D), 1.0, 6.0, ((0, 16),))
    norm_gain = jnp.clip(1.0 + 0.1 * jax.random.normal(streams_of[1], (D,), jnp.float32), 0.5, 1.5)
    query_base = scatter_about(streams_of[2], (D, HQ * DH), D ** -0.5, 0.0625, ((0, 128),))
    key_base = scatter_about(streams_of[3], (D, KVH * DH), D ** -0.5, 0.0625, ((0, 128),))
    value_base = scatter_about(streams_of[4], (D, KVH * DH), D ** -0.5, 0.0625, ((0, 128),))
    output_base = scatter_about(streams_of[5], (HQ * DH, D), (HQ * DH // 64) ** -0.5, 0.5, ((0, 128),))
    query_down = scatter_about(streams_of[6], (SLOTS, D, R), D ** -0.5, 0.0625, ((1, 128),))
    query_up = scatter_about(streams_of[7], (SLOTS, R, HQ * DH), R ** -0.5, 0.75)
    key_down = scatter_about(streams_of[8], (SLOTS, D, R), D ** -0.5, 0.0625, ((1, 128),))
    key_up = scatter_about(streams_of[9], (SLOTS, R, KVH * DH), R ** -0.5, 0.75)
    value_down = scatter_about(streams_of[10], (SLOTS, D, R), D ** -0.5, 0.0625, ((1, 128),))
    value_up = scatter_about(streams_of[11], (SLOTS, R, KVH * DH), R ** -0.5, 0.75)
    output_down = scatter_about(streams_of[12], (SLOTS, HQ * DH, R), (HQ * DH // 64) ** -0.5, 0.5, ((1, 128),))
    output_up = scatter_about(streams_of[13], (SLOTS, R, D), R ** -0.5, 0.75)
    adapter_layer = jax.random.randint(streams_of[14], (1,), 0, SLOTS).astype(jnp.int32)
    kv_lengths = plant(jax.random.randint(streams_of[15], (SEQS,), 8, LEN + 1), jax.random.fold_in(streams_of[15], 1), 8, LEN).astype(jnp.int32)
    cache_keys = draw_cache_keys(jax.random.fold_in(streams_of[18], 71), 0)
    cache_values = scatter_about(streams_of[17], (SEQS, LEN, KVH, DH), 1.0, 6.0, ((0, 16), (2, 8)))
    return dict(states=states, norm_gain=norm_gain, query_base=query_base, key_base=key_base, value_base=value_base, output_base=output_base, query_down=query_down, query_up=query_up, key_down=key_down, key_up=key_up, value_down=value_down, value_up=value_up, output_down=output_down, output_up=output_up, adapter_layer=adapter_layer, kv_lengths=kv_lengths, cache_keys=cache_keys, cache_values=cache_values)


rope_theta = 1000000.0
low_rank_scale = 0.5
epsilon = 1e-06

def merge_rows(frozen_base_rows, down_stack, up_stack, adapter_slot):
    down_rows = lax.dynamic_index_in_dim(down_stack, adapter_slot, 0, keepdims=False)
    up_projection_rows = lax.dynamic_index_in_dim(up_stack, adapter_slot, 0, keepdims=False)
    low_rank_delta = jnp.dot(down_rows, up_projection_rows, preferred_element_type=jnp.float32)
    return (frozen_base_rows.astype(jnp.float32) + low_rank_scale * low_rank_delta).astype(jnp.bfloat16)

def normalize(states, norm_gain):
    widened = states.astype(jnp.float32)
    squared_average = lax.optimization_barrier(jnp.mean(widened * widened, axis=-1, keepdims=True))
    return (widened * lax.rsqrt(squared_average + epsilon) * norm_gain).astype(jnp.bfloat16)

def rotate(vectors, positions):
    head_dim = vectors.shape[-1]
    half_dim = head_dim // 2
    frequency = rope_theta ** (-2.0 * jnp.arange(half_dim, dtype=jnp.float32) / head_dim)
    rotation_phases = positions[:, :, None] * frequency[None, None, :]
    cosine_table = jnp.concatenate((jnp.cos(rotation_phases), jnp.cos(rotation_phases)), -1)[:, :, None, :]
    sine_table = jnp.concatenate((jnp.sin(rotation_phases), jnp.sin(rotation_phases)), -1)[:, :, None, :]
    turned = jnp.concatenate((-vectors[..., half_dim:], vectors[..., :half_dim]), -1)
    return vectors * cosine_table + turned * sine_table

def attend_block(inputs):
    queries, keys_new, values_new, cache_k, cache_v, lengths = inputs
    seq_count, step_count, head_count, head_dim = queries.shape
    kv_count = keys_new.shape[2]
    grouped = queries.astype(jnp.float32).reshape(seq_count, step_count, kv_count, head_count // kv_count, head_dim)
    score_scale = head_dim ** (-0.5)
    old_scores = jnp.einsum('bskgd,blkd->bskgl', grouped, cache_k.astype(jnp.float32)) * score_scale
    new_scores = jnp.einsum('bskgd,btkd->bskgt', grouped, keys_new.astype(jnp.float32)) * score_scale
    live_slots = jnp.arange(cache_k.shape[1], dtype=jnp.int32)[None, :] < lengths[:, None]
    old_scores = jnp.where(live_slots[:, None, None, None, :], old_scores, -1e+30)
    causal = jnp.arange(step_count)[:, None] >= jnp.arange(step_count)[None, :]
    new_scores = jnp.where(causal[None, :, None, None, :], new_scores, -1e+30)
    highest = jnp.maximum(lax.optimization_barrier(jnp.max(old_scores, -1)), lax.optimization_barrier(jnp.max(new_scores, -1)))[..., None]
    old_exp = jnp.exp(old_scores - highest)
    new_exp = jnp.exp(new_scores - highest)
    denominator = lax.optimization_barrier(jnp.sum(old_exp, -1, keepdims=True)) + lax.optimization_barrier(jnp.sum(new_exp, -1, keepdims=True))
    old_weights = (old_exp / denominator).astype(jnp.bfloat16)
    new_weights = (new_exp / denominator).astype(jnp.bfloat16)
    mixture = jnp.einsum('bskgl,blkd->bskgd', old_weights.astype(jnp.float32), cache_v.astype(jnp.float32))
    mixture = mixture + jnp.einsum('bskgt,btkd->bskgd', new_weights.astype(jnp.float32), values_new.astype(jnp.float32))
    return mixture.astype(jnp.bfloat16).reshape(seq_count, step_count, head_count * head_dim)

def blockwise(tensor):
    return tensor.reshape((N_FSDP, SEQ_DEV) + tensor.shape[1:])

def reference(states, norm_gain, query_base, key_base, value_base, output_base, query_down, query_up, key_down, key_up, value_down, value_up, output_down, output_up, adapter_layer, kv_lengths, cache_keys, cache_values):
    adapter_slot = adapter_layer[0]
    merged_query = merge_rows(query_base, query_down, query_up, adapter_slot)
    merged_key = merge_rows(key_base, key_down, key_up, adapter_slot)
    merged_value = merge_rows(value_base, value_down, value_up, adapter_slot)
    merged_output = merge_rows(output_base, output_down, output_up, adapter_slot)
    normed = normalize(states, norm_gain)
    flat_rows = normed.reshape(SEQS * STEPS, D)
    positions = kv_lengths.astype(jnp.float32)[:, None] + jnp.arange(STEPS, dtype=jnp.float32)[None, :]
    queries = jnp.dot(flat_rows, merged_query, preferred_element_type=jnp.float32).reshape(SEQS, STEPS, HQ, DH)
    queries = rotate(queries, positions).astype(jnp.bfloat16)
    keys_new = jnp.dot(flat_rows, merged_key, preferred_element_type=jnp.float32).reshape(SEQS, STEPS, KVH, DH)
    keys_new = rotate(keys_new, positions).astype(jnp.bfloat16)
    values_new = jnp.dot(flat_rows, merged_value, preferred_element_type=jnp.float32).reshape(SEQS, STEPS, KVH, DH).astype(jnp.bfloat16)
    attended = lax.map(attend_block, (blockwise(queries), blockwise(keys_new), blockwise(values_new), blockwise(cache_keys), blockwise(cache_values), blockwise(kv_lengths)))
    attended = attended.reshape(SEQS * STEPS, HQ * DH)
    layer_update = jnp.dot(attended, merged_output, preferred_element_type=jnp.float32)
    return layer_update.reshape(SEQS, STEPS, D).astype(jnp.bfloat16)
```

```python
import functools

import jax
import jax.numpy as jnp
from jax import lax
from jax.experimental import pallas as pl
from jax.experimental.pallas import tpu as pltpu
from jax.sharding import PartitionSpec as P

HQ = 64
KVH = 8
DH = 128
MESH = pl.DeviceIdType.MESH

rope_theta = 1000000.0
low_rank_scale = 0.5
epsilon = 1e-06

TOK = 128
WROWS = 64
PLANE = 2048
QKV = 1280
OUT = 1024
CW = 256
NC = QKV // CW
NO = OUT // CW


def coords():
    f = lax.axis_index("fsdp")
    t = lax.axis_index("tp")
    return f // 4, lax.rem(f // 2, 2), lax.rem(f, 2), t


def flip(v, bit):
    return 1 - v if bit else v


def xor_z(z, e):
    hi, lo = z // 2, lax.rem(z, 2)
    return flip(hi, e >> 1) * 2 + flip(lo, e & 1)


def xor_t(t, d):
    b2, b1, b0 = t // 4, lax.rem(t // 2, 2), lax.rem(t, 2)
    return flip(b2, (d >> 2) & 1) * 4 + flip(b1, (d >> 1) & 1) * 2 + flip(b0, d & 1)


def dev(z, xl, c, t):
    return ((z * 2 + xl) * 2 + c, t)


def remote(src, dst, ssem, rsem, device):
    return pltpu.make_async_remote_copy(
        src_ref=src, dst_ref=dst, send_sem=ssem, recv_sem=rsem, device_id=device, device_id_type=MESH
    )


def project_kernel(
    a_ref, w_ref, o_ref, out_ref, wo_ref,
    abuf, wbuf, acc, crecv,
    a_ss, a_rs, w1_ss, w1_rs, w2_ss, w2_rs, w3_ss, w3_rs, c_ss, c_rs,
):
    z, xl, c, t = coords()
    xh = t // 4
    y4 = xh * 4
    xpart = dev(z, 1 - xl, c, t)
    cpart = dev(z, xl, 1 - c, t)

    def plane_peer(d):
        return dev(z, flip(xl, d >> 2), c, xor_t(t, d))

    def z_peer(e):
        return dev(xor_z(z, e), xl, c, t)

    barrier = pltpu.get_barrier_semaphore()
    peers = [plane_peer(d) for d in range(1, 8)] + [z_peer(e) for e in range(1, 4)] + [xpart, cpart]
    for p in peers:
        pl.semaphore_signal(barrier, inc=1, device_id=p, device_id_type=MESH)
    pl.semaphore_wait(barrier, len(peers))

    def a_copy(e):
        cols = pl.ds(pl.multiple_of(xor_z(z, e) * PLANE, PLANE), PLANE)
        if e == 0:
            return pltpu.make_async_copy(a_ref.at[:, cols], abuf.at[0], a_rs.at[0])
        return remote(a_ref.at[:, cols], abuf.at[e], a_ss.at[e], a_rs.at[e], z_peer(e))

    my_slot = (xl * 2 + c) * 8 + t

    def w1_copy(ch, d):
        td = xor_t(t, d)
        cols = pl.ds(pl.multiple_of(td * QKV + ch * CW, CW), CW)
        src = w_ref.at[:, cols]
        dst = wbuf.at[ch, my_slot]
        if d == 0:
            return pltpu.make_async_copy(src, dst, w1_rs.at[ch, 0])
        return remote(src, dst, w1_ss.at[ch, d], w1_rs.at[ch, d], plane_peer(d))

    def o1_copy(d):
        cols = pl.ds(pl.multiple_of(xor_t(t, d) * OUT, OUT), OUT)
        src = o_ref.at[:, cols]
        dst = wo_ref.at[my_slot]
        if d == 0:
            return pltpu.make_async_copy(src, dst, w1_rs.at[NC, 0])
        return remote(src, dst, w1_ss.at[NC, d], w1_rs.at[NC, d], plane_peer(d))

    def group_base(g, core):
        lo = xl if g in (0, 3) else 1 - xl
        hi = xh if g in (0, 2) else 1 - xh
        return (lo * 2 + core) * 8 + hi * 4

    def rows_of(k, base):
        if k is None:
            return wo_ref.at[pl.ds(base, 4)]
        return wbuf.at[k, pl.ds(base, 4)]

    def w2_copy(k, g):
        i = NC if k is None else k
        ref = rows_of(k, group_base(g, c))
        return remote(ref, ref, w2_ss.at[i, g], w2_rs.at[i, g], xpart)

    def w2_wait(k, g):
        i = NC if k is None else k
        ref = rows_of(k, group_base(g + 2, c))
        remote(ref, ref, w2_ss.at[i, g], w2_rs.at[i, g], xpart).wait_recv()

    def w3_copy(k, g):
        i = NC if k is None else k
        ref = rows_of(k, group_base(g, c))
        return remote(ref, ref, w3_ss.at[i, g], w3_rs.at[i, g], cpart)

    def w3_wait(k, g):
        i = NC if k is None else k
        ref = rows_of(k, group_base(g, 1 - c))
        remote(ref, ref, w3_ss.at[i, g], w3_rs.at[i, g], cpart).wait_recv()

    def c_copy(ch, e):
        return remote(acc.at[ch, e], crecv.at[ch, e - 1], c_ss.at[ch, e], c_rs.at[ch, e], z_peer(e))

    def start_w1(ch, carry):
        for d in range(8):
            w1_copy(ch, d).start()
        return carry

    start_w1(0, 0)
    for e in (1, 3, 2, 0):
        a_copy(e).start()
    lax.fori_loop(1, NC, start_w1, 0)
    for d in range(8):
        o1_copy(d).start()

    def gather(k, arrived):
        for g in range(2):
            for d in range(g * 4, g * 4 + 4):
                arrived(d)
            w2_copy(k, g).start()
            w3_copy(k, g).start()
        for g in range(2):
            w2_wait(k, g)
            w3_copy(k, g + 2).start()
        for g in range(4):
            w3_wait(k, g)

    def chunk(ch, carry):
        def arrived(d):
            if d == 0:
                w1_copy(ch, 0).wait()
            else:
                ref = wbuf.at[ch, (flip(xl, d >> 2) * 2 + c) * 8 + xor_t(t, d)]
                remote(ref, ref, w1_ss.at[ch, d], w1_rs.at[ch, d], plane_peer(d)).wait_recv()

        gather(ch, arrived)

        @pl.when(ch == 0)
        def _():
            a_copy(0).wait()
            for e in (1, 3, 2):
                a_copy(e).wait_recv()

        rows = abuf[...].reshape(4 * TOK, PLANE)
        part = jnp.dot(rows, wbuf[ch].reshape(PLANE, CW), preferred_element_type=jnp.float32)
        acc[ch] = part.reshape(4, TOK, CW)
        for e in (1, 3, 2):
            c_copy(ch, e).start()
        return carry

    lax.fori_loop(0, NC, chunk, 0)

    def arrived_o(d):
        if d == 0:
            o1_copy(0).wait()
        else:
            ref = wo_ref.at[(flip(xl, d >> 2) * 2 + c) * 8 + xor_t(t, d)]
            remote(ref, ref, w1_ss.at[NC, d], w1_rs.at[NC, d], plane_peer(d)).wait_recv()

    gather(None, arrived_o)

    for ch in range(NC):
        for e in range(1, 4):
            c_copy(ch, e).wait_recv()
        out_ref[:, ch * CW : (ch + 1) * CW] = acc[ch, 0] + crecv[ch, 0] + crecv[ch, 1] + crecv[ch, 2]

    for e in range(1, 4):
        a_copy(e).wait_send()

    def drain(ch, carry):
        for d in range(1, 8):
            w1_copy(ch, d).wait_send()
        for g in range(2):
            w2_copy(ch, g).wait_send()
        for g in range(4):
            w3_copy(ch, g).wait_send()
        for e in range(1, 4):
            c_copy(ch, e).wait_send()
        return carry

    lax.fori_loop(0, NC, drain, 0)
    for d in range(1, 8):
        o1_copy(d).wait_send()
    for g in range(2):
        w2_copy(None, g).wait_send()
    for g in range(4):
        w3_copy(None, g).wait_send()


def output_kernel(
    h_ref, wo_ref, out_ref,
    abuf, wbuf, acc, crecv,
    wl_s, a_ss, a_rs, c_ss, c_rs,
):
    z, xl, c, t = coords()
    zd = t // 2
    half = lax.rem(t, 2)

    def target(d):
        return dev(zd, xl, c, xor_t(t, d))

    def z_peer(e):
        return dev(xor_z(z, e), xl, c, t)

    slot = lax.rem(z // 2 + zd // 2, 2) * 2 + lax.rem(lax.rem(z, 2) + lax.rem(zd, 2), 2)
    here = z == zd

    def source(e, h):
        return dev(xor_z(z, e), xl, c, 2 * z + h)

    loads = [
        pltpu.make_async_copy(wo_ref, wbuf, wl_s.at[0]),
    ]
    for load in loads:
        load.start()

    barrier = pltpu.get_barrier_semaphore()
    count = 0
    for e in range(1, 4):
        pl.semaphore_signal(barrier, inc=1, device_id=z_peer(e), device_id_type=MESH)
    for d in range(8):
        pl.semaphore_signal(barrier, inc=1, device_id=target(d), device_id_type=MESH)
    for e in range(4):
        for h in range(2):
            pl.semaphore_signal(barrier, inc=1, device_id=source(e, h), device_id_type=MESH)
    pl.semaphore_wait(barrier, 3 + 8 + 8)

    def a_send(d):
        dst = abuf.at[slot, :, pl.ds(pl.multiple_of(half * OUT, OUT), OUT)]
        return remote(h_ref, dst, a_ss.at[d], a_rs.at[slot, half], target(d))

    def a_local():
        dst = abuf.at[0, :, pl.ds(pl.multiple_of(half * OUT, OUT), OUT)]
        return pltpu.make_async_copy(h_ref, dst, a_rs.at[0, half])

    @pl.when(here)
    def _():
        a_local().start()

    @pl.when(jnp.logical_not(here))
    def _():
        a_send(0).start()

    for d in range(1, 8):
        a_send(d).start()

    for e in range(4):
        for h in range(2):
            ref = abuf.at[e, :, pl.ds(h * OUT, OUT)]
            pltpu.make_async_copy(ref, ref, a_rs.at[e, h]).wait()
    for load in loads:
        load.wait()

    def c_copy(ch, e):
        return remote(acc.at[ch, e], crecv.at[ch, e - 1], c_ss.at[ch, e], c_rs.at[ch, e], z_peer(e))

    own = []
    for ch in range(NO):
        w = wbuf[:, :, ch * CW : (ch + 1) * CW].reshape(PLANE, CW)
        part = jnp.dot(abuf[...].reshape(4 * TOK, PLANE), w, preferred_element_type=jnp.float32)
        acc[ch] = part.reshape(4, TOK, CW)
        for e in (1, 3, 2):
            c_copy(ch, e).start()
    for ch in range(NO):
        for e in range(1, 4):
            c_copy(ch, e).wait_recv()
        total = acc[ch, 0] + crecv[ch, 0] + crecv[ch, 1] + crecv[ch, 2]
        out_ref[:, ch * CW : (ch + 1) * CW] = total.astype(jnp.bfloat16)

    @pl.when(jnp.logical_not(here))
    def _():
        a_send(0).wait_send()

    for d in range(1, 8):
        a_send(d).wait_send()
    for ch in range(NO):
        for e in range(1, 4):
            c_copy(ch, e).wait_send()


VM = pl.BlockSpec(memory_space=pltpu.VMEM)
ANY = pl.BlockSpec(memory_space=pl.ANY)
DMA = pltpu.SemaphoreType.DMA


def project(normed, joined, merged_output):
    return pl.pallas_call(
        project_kernel,
        out_shape=(
            jax.ShapeDtypeStruct((TOK, QKV), jnp.float32),
            jax.ShapeDtypeStruct((32, WROWS, OUT), jnp.bfloat16),
        ),
        in_specs=[VM, VM, ANY],
        out_specs=(VM, ANY),
        scratch_shapes=[
            pltpu.VMEM((4, TOK, PLANE), jnp.bfloat16),
            pltpu.VMEM((NC, 32, WROWS, CW), jnp.bfloat16),
            pltpu.VMEM((NC, 4, TOK, CW), jnp.float32),
            pltpu.VMEM((NC, 3, TOK, CW), jnp.float32),
            DMA((4,)), DMA((4,)),
            DMA((NC + 1, 8)), DMA((NC + 1, 8)),
            DMA((NC + 1, 2)), DMA((NC + 1, 2)),
            DMA((NC + 1, 4)), DMA((NC + 1, 4)),
            DMA((NC, 4)), DMA((NC, 4)),
        ],
        compiler_params=pltpu.CompilerParams(collective_id=0, has_side_effects=True, vmem_limit_bytes=48 << 20),
        name="project",
    )(normed, joined, merged_output)


def output_projection(heads, weights):
    return pl.pallas_call(
        output_kernel,
        out_shape=jax.ShapeDtypeStruct((TOK, OUT), jnp.bfloat16),
        in_specs=[VM, ANY],
        out_specs=VM,
        scratch_shapes=[
            pltpu.VMEM((4, TOK, PLANE), jnp.bfloat16),
            pltpu.VMEM((32, WROWS, OUT), jnp.bfloat16),
            pltpu.VMEM((NO, 4, TOK, CW), jnp.float32),
            pltpu.VMEM((NO, 3, TOK, CW), jnp.float32),
            DMA((1,)),
            DMA((8,)), DMA((4, 2)),
            DMA((NO, 4)), DMA((NO, 4)),
        ],
        compiler_params=pltpu.CompilerParams(collective_id=1, has_side_effects=True, vmem_limit_bytes=48 << 20),
        name="output_projection",
    )(heads, weights)


def merge_rows(frozen_base_rows, down_stack, up_stack, adapter_slot):
    down_rows = lax.dynamic_index_in_dim(down_stack, adapter_slot, 0, keepdims=False)
    up_projection_rows = lax.dynamic_index_in_dim(up_stack, adapter_slot, 0, keepdims=False)
    low_rank_delta = jnp.dot(down_rows, up_projection_rows, preferred_element_type=jnp.float32)
    return (frozen_base_rows.astype(jnp.float32) + low_rank_scale * low_rank_delta).astype(
        jnp.bfloat16
    )


def normalize(states, norm_gain):
    widened = states.astype(jnp.float32)
    squared_average = jnp.mean(widened * widened, axis=-1, keepdims=True)
    return (widened * lax.rsqrt(squared_average + epsilon) * norm_gain).astype(jnp.bfloat16)


def rotate(vectors, positions):
    head_dim = vectors.shape[-1]
    half_dim = head_dim // 2
    frequency = rope_theta ** (-2.0 * jnp.arange(half_dim, dtype=jnp.float32) / head_dim)
    rotation_phases = positions[:, :, None] * frequency[None, None, :]
    cosine_table = jnp.concatenate((jnp.cos(rotation_phases), jnp.cos(rotation_phases)), -1)[
        :, :, None, :
    ]
    sine_table = jnp.concatenate((jnp.sin(rotation_phases), jnp.sin(rotation_phases)), -1)[
        :, :, None, :
    ]
    turned = jnp.concatenate((-vectors[..., half_dim:], vectors[..., :half_dim]), -1)
    return vectors * cosine_table + turned * sine_table


def attend(queries, keys_new, values_new, cache_k, cache_v, lengths):
    seq_count, step_count, head_count, head_dim = queries.shape
    kv_count = keys_new.shape[2]
    grouped = queries.reshape(seq_count, step_count, kv_count, head_count // kv_count, head_dim)
    score_scale = head_dim ** (-0.5)
    old_scores = (
        jnp.einsum("bskgd,blkd->bskgl", grouped, cache_k, preferred_element_type=jnp.float32)
        * score_scale
    )
    new_scores = (
        jnp.einsum("bskgd,btkd->bskgt", grouped, keys_new, preferred_element_type=jnp.float32)
        * score_scale
    )
    live_slots = jnp.arange(cache_k.shape[1], dtype=jnp.int32)[None, :] < lengths[:, None]
    old_scores = jnp.where(live_slots[:, None, None, None, :], old_scores, -1e30)
    causal = jnp.arange(step_count)[:, None] >= jnp.arange(step_count)[None, :]
    new_scores = jnp.where(causal[None, :, None, None, :], new_scores, -1e30)
    highest = jnp.maximum(jnp.max(old_scores, -1), jnp.max(new_scores, -1))[..., None]
    old_exp = jnp.exp(old_scores - highest)
    new_exp = jnp.exp(new_scores - highest)
    denominator = jnp.sum(old_exp, -1, keepdims=True) + jnp.sum(new_exp, -1, keepdims=True)
    old_weights = (old_exp / denominator).astype(jnp.bfloat16)
    new_weights = (new_exp / denominator).astype(jnp.bfloat16)
    mixture = jnp.einsum(
        "bskgl,blkd->bskgd", old_weights, cache_v, preferred_element_type=jnp.float32
    )
    mixture = mixture + jnp.einsum(
        "bskgt,btkd->bskgd", new_weights, values_new, preferred_element_type=jnp.float32
    )
    return mixture.astype(jnp.bfloat16).reshape(seq_count, step_count, head_count * head_dim)


def local(
    states,
    norm_gain,
    query_base,
    key_base,
    value_base,
    output_base,
    query_down,
    query_up,
    key_down,
    key_up,
    value_down,
    value_up,
    output_down,
    output_up,
    adapter_layer,
    kv_lengths,
    cache_keys,
    cache_values,
):
    adapter_slot = adapter_layer[0]
    tp_size = lax.axis_size("tp")
    row_count = query_base.shape[0]
    merged_query = merge_rows(query_base, query_down, query_up, adapter_slot)
    merged_key = merge_rows(key_base, key_down, key_up, adapter_slot)
    merged_value = merge_rows(value_base, value_down, value_up, adapter_slot)
    merged_output = merge_rows(output_base, output_down, output_up, adapter_slot)
    joined = jnp.concatenate(
        (
            merged_query.reshape(row_count, tp_size, -1),
            merged_key.reshape(row_count, tp_size, -1),
            merged_value.reshape(row_count, tp_size, -1),
        ),
        2,
    ).reshape(row_count, -1)
    seq_count, step_count, model_width = states.shape
    normed = normalize(states, norm_gain).reshape(seq_count * step_count, model_width)
    projected, output_rows = project(normed, joined, merged_output)
    head_cols = HQ * DH // tp_size
    kv_cols = KVH * DH // tp_size
    projected = projected.reshape(seq_count, step_count, -1)
    positions = (
        kv_lengths.astype(jnp.float32)[:, None] + jnp.arange(step_count, dtype=jnp.float32)[None, :]
    )
    queries = rotate(
        projected[:, :, :head_cols].reshape(seq_count, step_count, -1, DH), positions
    ).astype(jnp.bfloat16)
    keys_new = rotate(
        projected[:, :, head_cols : head_cols + kv_cols].reshape(seq_count, step_count, -1, DH),
        positions,
    ).astype(jnp.bfloat16)
    values_new = (
        projected[:, :, head_cols + kv_cols :]
        .reshape(seq_count, step_count, -1, DH)
        .astype(jnp.bfloat16)
    )
    attended = attend(queries, keys_new, values_new, cache_keys, cache_values, kv_lengths)
    update = output_projection(attended.reshape(seq_count * step_count, -1), output_rows)
    return update.reshape(seq_count, step_count, -1)


def solution(mesh):
    in_specs = (
        P("fsdp", None, None),
        P(),
        P(("fsdp", "tp"), None),
        P(("fsdp", "tp"), None),
        P(("fsdp", "tp"), None),
        P(("fsdp", "tp"), None),
        P(None, ("fsdp", "tp"), None),
        P(),
        P(None, ("fsdp", "tp"), None),
        P(),
        P(None, ("fsdp", "tp"), None),
        P(),
        P(None, ("fsdp", "tp"), None),
        P(),
        P(),
        P("fsdp"),
        P("fsdp", None, "tp", None),
        P("fsdp", None, "tp", None),
    )
    out_specs = P("fsdp", None, "tp")
    return jax.shard_map(local, mesh=mesh, in_specs=in_specs, out_specs=out_specs, check_vma=False)
```

```python
import functools

import jax
import jax.numpy as jnp
from jax import lax
from jax.experimental import pallas as pl
from jax.experimental.pallas import tpu as pltpu
from jax.sharding import PartitionSpec as P

HQ = 64
KVH = 8
DH = 128
MESH = pl.DeviceIdType.MESH

rope_theta = 1000000.0
low_rank_scale = 0.5
epsilon = 1e-06

TOK = 128
WROWS = 64
PLANE = 2048
QKV = 1280
OUT = 1024
CW = 256
NC = QKV // CW
NO = OUT // CW


def coords():
    f = lax.axis_index("fsdp")
    t = lax.axis_index("tp")
    return f // 4, lax.rem(f // 2, 2), lax.rem(f, 2), t


def flip(v, bit):
    return 1 - v if bit else v


def xor_z(z, e):
    hi, lo = z // 2, lax.rem(z, 2)
    return flip(hi, e >> 1) * 2 + flip(lo, e & 1)


def xor_t(t, d):
    b2, b1, b0 = t // 4, lax.rem(t // 2, 2), lax.rem(t, 2)
    return flip(b2, (d >> 2) & 1) * 4 + flip(b1, (d >> 1) & 1) * 2 + flip(b0, d & 1)


def dev(z, xl, c, t):
    return ((z * 2 + xl) * 2 + c, t)


def remote(src, dst, ssem, rsem, device):
    return pltpu.make_async_remote_copy(
        src_ref=src, dst_ref=dst, send_sem=ssem, recv_sem=rsem, device_id=device, device_id_type=MESH
    )


def project_kernel(
    a_ref, w_ref, o_ref, out_ref, wo_ref,
    abuf, wbuf, acc, crecv,
    a_ss, a_rs, w1_ss, w1_rs, w2_ss, w2_rs, w3_ss, w3_rs, c_ss, c_rs,
):
    z, xl, c, t = coords()
    xh = t // 4
    y4 = xh * 4
    xpart = dev(z, 1 - xl, c, t)
    cpart = dev(z, xl, 1 - c, t)

    def plane_peer(d):
        return dev(z, flip(xl, d >> 2), c, xor_t(t, d))

    def z_peer(e):
        return dev(xor_z(z, e), xl, c, t)

    barrier = pltpu.get_barrier_semaphore()
    peers = [plane_peer(d) for d in range(1, 8)] + [z_peer(e) for e in range(1, 4)] + [xpart, cpart]
    for p in peers:
        pl.semaphore_signal(barrier, inc=1, device_id=p, device_id_type=MESH)
    pl.semaphore_wait(barrier, len(peers))

    def a_copy(e):
        cols = pl.ds(pl.multiple_of(xor_z(z, e) * PLANE, PLANE), PLANE)
        if e == 0:
            return pltpu.make_async_copy(a_ref.at[:, cols], abuf.at[0], a_rs.at[0])
        return remote(a_ref.at[:, cols], abuf.at[e], a_ss.at[e], a_rs.at[e], z_peer(e))

    my_slot = (xl * 2 + c) * 8 + t

    def w1_copy(ch, d):
        td = xor_t(t, d)
        cols = pl.ds(pl.multiple_of(td * QKV + ch * CW, CW), CW)
        src = w_ref.at[:, cols]
        dst = wbuf.at[ch, my_slot]
        if d == 0:
            return pltpu.make_async_copy(src, dst, w1_rs.at[ch, 0])
        return remote(src, dst, w1_ss.at[ch, d], w1_rs.at[ch, d], plane_peer(d))

    def o1_copy(d):
        cols = pl.ds(pl.multiple_of(xor_t(t, d) * OUT, OUT), OUT)
        src = o_ref.at[:, cols]
        dst = wo_ref.at[my_slot]
        if d == 0:
            return pltpu.make_async_copy(src, dst, w1_rs.at[NC, 0])
        return remote(src, dst, w1_ss.at[NC, d], w1_rs.at[NC, d], plane_peer(d))

    def group_base(g, core):
        lo = xl if g in (0, 3) else 1 - xl
        hi = xh if g in (0, 2) else 1 - xh
        return (lo * 2 + core) * 8 + hi * 4

    def rows_of(k, base):
        if k is None:
            return wo_ref.at[pl.ds(base, 4)]
        return wbuf.at[k, pl.ds(base, 4)]

    def w2_copy(k, g):
        i = NC if k is None else k
        ref = rows_of(k, group_base(g, c))
        return remote(ref, ref, w2_ss.at[i, g], w2_rs.at[i, g], xpart)

    def w2_wait(k, g):
        i = NC if k is None else k
        ref = rows_of(k, group_base(g + 2, c))
        remote(ref, ref, w2_ss.at[i, g], w2_rs.at[i, g], xpart).wait_recv()

    def w3_copy(k, g):
        i = NC if k is None else k
        ref = rows_of(k, group_base(g, c))
        return remote(ref, ref, w3_ss.at[i, g], w3_rs.at[i, g], cpart)

    def w3_wait(k, g):
        i = NC if k is None else k
        ref = rows_of(k, group_base(g, 1 - c))
        remote(ref, ref, w3_ss.at[i, g], w3_rs.at[i, g], cpart).wait_recv()

    def c_copy(ch, e):
        return remote(acc.at[ch, e], crecv.at[ch, e - 1], c_ss.at[ch, e], c_rs.at[ch, e], z_peer(e))

    def start_w1(ch, carry):
        for d in range(8):
            w1_copy(ch, d).start()
        return carry

    start_w1(0, 0)
    for e in (1, 3, 2, 0):
        a_copy(e).start()
    lax.fori_loop(1, NC, start_w1, 0)
    for d in range(8):
        o1_copy(d).start()

    def relay(k):
        for g in range(2):
            for d in range(g * 4, g * 4 + 4):
                source_slot = (flip(xl, d >> 2) * 2 + c) * 8 + xor_t(t, d)
                if d == 0:
                    (o1_copy(0) if k is None else w1_copy(k, 0)).wait()
                elif k is None:
                    ref = wo_ref.at[source_slot]
                    remote(ref, ref, w1_ss.at[NC, d], w1_rs.at[NC, d], plane_peer(d)).wait_recv()
                else:
                    ref = wbuf.at[k, source_slot]
                    remote(ref, ref, w1_ss.at[k, d], w1_rs.at[k, d], plane_peer(d)).wait_recv()
            w2_copy(k, g).start()
            w3_copy(k, g).start()

    def share(k):
        for g in range(2):
            w2_wait(k, g)
            w3_copy(k, g + 2).start()

    def multiply(ch):
        for g in range(4):
            w3_wait(ch, g)
        rows = abuf[...].reshape(4 * TOK, PLANE)
        part = jnp.dot(rows, wbuf[ch].reshape(PLANE, CW), preferred_element_type=jnp.float32)
        acc[ch] = part.reshape(4, TOK, CW)
        for e in (1, 3, 2):
            c_copy(ch, e).start()

    relay(0)
    for ch in range(3):
        relay(ch + 1)
        share(ch)
    a_copy(0).wait()
    for e in (1, 3, 2):
        a_copy(e).wait_recv()
    multiply(0)
    relay(4)
    share(3)
    multiply(1)
    relay(None)
    share(4)
    for ch in range(2, NC):
        multiply(ch)
    share(None)
    for g in range(4):
        w3_wait(None, g)

    for ch in range(NC):
        for e in range(1, 4):
            c_copy(ch, e).wait_recv()
        out_ref[:, ch * CW : (ch + 1) * CW] = acc[ch, 0] + crecv[ch, 0] + crecv[ch, 1] + crecv[ch, 2]

    for e in range(1, 4):
        a_copy(e).wait_send()

    def drain(ch, carry):
        for d in range(1, 8):
            w1_copy(ch, d).wait_send()
        for g in range(2):
            w2_copy(ch, g).wait_send()
        for g in range(4):
            w3_copy(ch, g).wait_send()
        for e in range(1, 4):
            c_copy(ch, e).wait_send()
        return carry

    lax.fori_loop(0, NC, drain, 0)
    for d in range(1, 8):
        o1_copy(d).wait_send()
    for g in range(2):
        w2_copy(None, g).wait_send()
    for g in range(4):
        w3_copy(None, g).wait_send()


def output_kernel(
    h_ref, wo_ref, out_ref,
    abuf, wbuf, own, csend, crecv,
    wl_s, a_ss, a_rs, c_ss, c_rs,
):
    z, xl, c, t = coords()
    zd = t // 2
    half = lax.rem(t, 2)

    def target(d):
        return dev(zd, xl, c, xor_t(t, d))

    def z_peer(e):
        return dev(xor_z(z, e), xl, c, t)

    slot = lax.rem(z // 2 + zd // 2, 2) * 2 + lax.rem(lax.rem(z, 2) + lax.rem(zd, 2), 2)
    here = z == zd

    def source(e, h):
        return dev(xor_z(z, e), xl, c, 2 * z + h)

    loads = [
        pltpu.make_async_copy(wo_ref, wbuf, wl_s.at[0]),
    ]
    for load in loads:
        load.start()

    barrier = pltpu.get_barrier_semaphore()
    count = 0
    for e in range(1, 4):
        pl.semaphore_signal(barrier, inc=1, device_id=z_peer(e), device_id_type=MESH)
    for d in range(8):
        pl.semaphore_signal(barrier, inc=1, device_id=target(d), device_id_type=MESH)
    for e in range(4):
        for h in range(2):
            pl.semaphore_signal(barrier, inc=1, device_id=source(e, h), device_id_type=MESH)
    pl.semaphore_wait(barrier, 3 + 8 + 8)

    def a_send(d):
        dst = abuf.at[slot, :, pl.ds(pl.multiple_of(half * OUT, OUT), OUT)]
        return remote(h_ref, dst, a_ss.at[d], a_rs.at[slot, half], target(d))

    def a_local():
        dst = abuf.at[0, :, pl.ds(pl.multiple_of(half * OUT, OUT), OUT)]
        return pltpu.make_async_copy(h_ref, dst, a_rs.at[0, half])

    for d in (4, 1):
        a_send(d).start()

    @pl.when(here)
    def _():
        a_local().start()

    @pl.when(jnp.logical_not(here))
    def _():
        a_send(0).start()

    for d in (6, 3, 5, 2, 7):
        a_send(d).start()

    for e in range(4):
        for h in range(2):
            ref = abuf.at[e, :, pl.ds(h * OUT, OUT)]
            pltpu.make_async_copy(ref, ref, a_rs.at[e, h]).wait()
    for load in loads:
        load.wait()

    def c_copy(ch, e):
        return remote(csend.at[ch, e - 1], crecv.at[ch, e - 1], c_ss.at[ch, e], c_rs.at[ch, e], z_peer(e))

    for ch in range(NO):
        w = wbuf[:, :, ch * CW : (ch + 1) * CW].reshape(PLANE, CW)
        part = jnp.dot(abuf[...].reshape(4 * TOK, PLANE), w, preferred_element_type=jnp.float32)
        own[ch] = part[:TOK]
        csend[ch] = part[TOK:].astype(jnp.bfloat16).reshape(3, TOK, CW)
        for e in (1, 3, 2):
            c_copy(ch, e).start()
    for ch in range(NO):
        for e in range(1, 4):
            c_copy(ch, e).wait_recv()
        total = own[ch]
        for e in range(3):
            total = total + crecv[ch, e].astype(jnp.float32)
        out_ref[:, ch * CW : (ch + 1) * CW] = total.astype(jnp.bfloat16)

    @pl.when(jnp.logical_not(here))
    def _():
        a_send(0).wait_send()

    for d in range(1, 8):
        a_send(d).wait_send()
    for ch in range(NO):
        for e in range(1, 4):
            c_copy(ch, e).wait_send()


VM = pl.BlockSpec(memory_space=pltpu.VMEM)
ANY = pl.BlockSpec(memory_space=pl.ANY)
DMA = pltpu.SemaphoreType.DMA


def project(normed, joined, merged_output):
    return pl.pallas_call(
        project_kernel,
        out_shape=(
            jax.ShapeDtypeStruct((TOK, QKV), jnp.float32),
            jax.ShapeDtypeStruct((32, WROWS, OUT), jnp.bfloat16),
        ),
        in_specs=[ANY, ANY, ANY],
        out_specs=(VM, ANY),
        scratch_shapes=[
            pltpu.VMEM((4, TOK, PLANE), jnp.bfloat16),
            pltpu.VMEM((NC, 32, WROWS, CW), jnp.bfloat16),
            pltpu.VMEM((NC, 4, TOK, CW), jnp.float32),
            pltpu.VMEM((NC, 3, TOK, CW), jnp.float32),
            DMA((4,)), DMA((4,)),
            DMA((NC + 1, 8)), DMA((NC + 1, 8)),
            DMA((NC + 1, 2)), DMA((NC + 1, 2)),
            DMA((NC + 1, 4)), DMA((NC + 1, 4)),
            DMA((NC, 4)), DMA((NC, 4)),
        ],
        compiler_params=pltpu.CompilerParams(collective_id=0, has_side_effects=True, vmem_limit_bytes=48 << 20),
        name="project",
    )(normed, joined, merged_output)


def output_projection(heads, weights):
    return pl.pallas_call(
        output_kernel,
        out_shape=jax.ShapeDtypeStruct((TOK, OUT), jnp.bfloat16),
        in_specs=[VM, ANY],
        out_specs=VM,
        scratch_shapes=[
            pltpu.VMEM((4, TOK, PLANE), jnp.bfloat16),
            pltpu.VMEM((32, WROWS, OUT), jnp.bfloat16),
            pltpu.VMEM((NO, TOK, CW), jnp.float32),
            pltpu.VMEM((NO, 3, TOK, CW), jnp.bfloat16),
            pltpu.VMEM((NO, 3, TOK, CW), jnp.bfloat16),
            DMA((1,)),
            DMA((8,)), DMA((4, 2)),
            DMA((NO, 4)), DMA((NO, 4)),
        ],
        compiler_params=pltpu.CompilerParams(collective_id=1, has_side_effects=True, vmem_limit_bytes=48 << 20),
        name="output_projection",
    )(heads, weights)


def prepare_kernel(
    slot_ref, gain_ref, states_ref, q_ref, k_ref, v_ref, o_ref,
    qd_ref, kd_ref, vd_ref, od_ref, qu_ref, ku_ref, vu_ref, ou_ref,
    normed_ref, joined_ref, merged_ref,
):
    def merge(base, down, up):
        delta = jnp.dot(down[0], up[0], preferred_element_type=jnp.float32)
        return (base[...].astype(jnp.float32) + low_rank_scale * delta).astype(jnp.bfloat16)

    head_cols = q_ref.shape[1]
    kv_cols = k_ref.shape[1]
    joined_ref[:, :head_cols] = merge(q_ref, qd_ref, qu_ref)
    joined_ref[:, head_cols : head_cols + kv_cols] = merge(k_ref, kd_ref, ku_ref)
    joined_ref[:, head_cols + kv_cols :] = merge(v_ref, vd_ref, vu_ref)
    merged_ref[...] = merge(o_ref, od_ref, ou_ref)
    widened = states_ref[...].astype(jnp.float32)
    squared_average = jnp.mean(widened * widened, axis=-1, keepdims=True)
    normed = widened * lax.rsqrt(squared_average + epsilon) * gain_ref[...].reshape(1, 1, -1)
    normed_ref[...] = normed.reshape(normed_ref.shape).astype(jnp.bfloat16)


def prepare(slot, gain, states, bases, downs, ups):
    steps = 8
    seqs, decode, width = states.shape
    block = seqs // steps

    def cols(array):
        return pl.BlockSpec((array.shape[0], array.shape[1] // steps), lambda i, s: (0, i))

    def down(array):
        return pl.BlockSpec((1, *array.shape[1:]), lambda i, s: (s[0], 0, 0))

    def up(array):
        return pl.BlockSpec((1, array.shape[1], array.shape[2] // steps), lambda i, s: (s[0], 0, i))

    return pl.pallas_call(
        prepare_kernel,
        out_shape=(
            jax.ShapeDtypeStruct((seqs * decode, width), jnp.bfloat16),
            jax.ShapeDtypeStruct((WROWS, QKV * steps), jnp.bfloat16),
            jax.ShapeDtypeStruct((WROWS, OUT * steps), jnp.bfloat16),
        ),
        grid_spec=pltpu.PrefetchScalarGridSpec(
            num_scalar_prefetch=1,
            grid=(steps,),
            in_specs=[
                pl.BlockSpec((1, width), lambda i, s: (0, 0)),
                pl.BlockSpec((block, decode, width), lambda i, s: (i, 0, 0)),
                *[cols(b) for b in bases],
                *[down(d) for d in downs],
                *[up(u) for u in ups],
            ],
            out_specs=(
                pl.BlockSpec((block * decode, width), lambda i, s: (i, 0)),
                pl.BlockSpec((WROWS, QKV), lambda i, s: (0, i)),
                pl.BlockSpec((WROWS, OUT), lambda i, s: (0, i)),
            ),
        ),
        name="prepare",
    )(slot, gain.reshape(1, -1), states, *bases, *downs, *ups)


def rotate(vectors, positions):
    head_dim = vectors.shape[-1]
    half_dim = head_dim // 2
    frequency = rope_theta ** (-2.0 * jnp.arange(half_dim, dtype=jnp.float32) / head_dim)
    rotation_phases = positions[:, :, None] * frequency[None, None, :]
    cosine_table = jnp.concatenate((jnp.cos(rotation_phases), jnp.cos(rotation_phases)), -1)[
        :, :, None, :
    ]
    sine_table = jnp.concatenate((jnp.sin(rotation_phases), jnp.sin(rotation_phases)), -1)[
        :, :, None, :
    ]
    turned = jnp.concatenate((-vectors[..., half_dim:], vectors[..., :half_dim]), -1)
    return vectors * cosine_table + turned * sine_table


def attend(queries, keys_new, values_new, cache_k, cache_v, lengths):
    seq_count, step_count, head_count, head_dim = queries.shape
    kv_count = keys_new.shape[2]
    grouped = queries.reshape(seq_count, step_count, kv_count, head_count // kv_count, head_dim)
    score_scale = head_dim ** (-0.5)
    old_scores = (
        jnp.einsum("bskgd,blkd->bskgl", grouped, cache_k, preferred_element_type=jnp.float32)
        * score_scale
    )
    new_scores = (
        jnp.einsum("bskgd,btkd->bskgt", grouped, keys_new, preferred_element_type=jnp.float32)
        * score_scale
    )
    live_slots = jnp.arange(cache_k.shape[1], dtype=jnp.int32)[None, :] < lengths[:, None]
    old_scores = jnp.where(live_slots[:, None, None, None, :], old_scores, -1e30)
    causal = jnp.arange(step_count)[:, None] >= jnp.arange(step_count)[None, :]
    new_scores = jnp.where(causal[None, :, None, None, :], new_scores, -1e30)
    highest = jnp.maximum(jnp.max(old_scores, -1), jnp.max(new_scores, -1))[..., None]
    old_exp = jnp.exp(old_scores - highest)
    new_exp = jnp.exp(new_scores - highest)
    denominator = jnp.sum(old_exp, -1, keepdims=True) + jnp.sum(new_exp, -1, keepdims=True)
    old_weights = (old_exp / denominator).astype(jnp.bfloat16)
    new_weights = (new_exp / denominator).astype(jnp.bfloat16)
    mixture = jnp.einsum(
        "bskgl,blkd->bskgd", old_weights, cache_v, preferred_element_type=jnp.float32
    )
    mixture = mixture + jnp.einsum(
        "bskgt,btkd->bskgd", new_weights, values_new, preferred_element_type=jnp.float32
    )
    return mixture.astype(jnp.bfloat16).reshape(seq_count, step_count, head_count * head_dim)


def local(
    states,
    norm_gain,
    query_base,
    key_base,
    value_base,
    output_base,
    query_down,
    query_up,
    key_down,
    key_up,
    value_down,
    value_up,
    output_down,
    output_up,
    adapter_layer,
    kv_lengths,
    cache_keys,
    cache_values,
):
    tp_size = lax.axis_size("tp")
    seq_count, step_count, _ = states.shape
    normed, joined, merged_output = prepare(
        adapter_layer,
        norm_gain,
        states,
        (query_base, key_base, value_base, output_base),
        (query_down, key_down, value_down, output_down),
        (query_up, key_up, value_up, output_up),
    )
    projected, output_rows = project(normed, joined, merged_output)
    head_cols = HQ * DH // tp_size
    kv_cols = KVH * DH // tp_size
    projected = projected.reshape(seq_count, step_count, -1)
    positions = (
        kv_lengths.astype(jnp.float32)[:, None] + jnp.arange(step_count, dtype=jnp.float32)[None, :]
    )
    queries = rotate(
        projected[:, :, :head_cols].reshape(seq_count, step_count, -1, DH), positions
    ).astype(jnp.bfloat16)
    keys_new = rotate(
        projected[:, :, head_cols : head_cols + kv_cols].reshape(seq_count, step_count, -1, DH),
        positions,
    ).astype(jnp.bfloat16)
    values_new = (
        projected[:, :, head_cols + kv_cols :]
        .reshape(seq_count, step_count, -1, DH)
        .astype(jnp.bfloat16)
    )
    attended = attend(queries, keys_new, values_new, cache_keys, cache_values, kv_lengths)
    update = output_projection(attended.reshape(seq_count * step_count, -1), output_rows)
    return update.reshape(seq_count, step_count, -1)


def solution(mesh):
    in_specs = (
        P("fsdp", None, None),
        P(),
        P(("fsdp", "tp"), None),
        P(("fsdp", "tp"), None),
        P(("fsdp", "tp"), None),
        P(("fsdp", "tp"), None),
        P(None, ("fsdp", "tp"), None),
        P(),
        P(None, ("fsdp", "tp"), None),
        P(),
        P(None, ("fsdp", "tp"), None),
        P(),
        P(None, ("fsdp", "tp"), None),
        P(),
        P(),
        P("fsdp"),
        P("fsdp", None, "tp", None),
        P("fsdp", None, "tp", None),
    )
    out_specs = P("fsdp", None, "tp")
    return jax.shard_map(local, mesh=mesh, in_specs=in_specs, out_specs=out_specs, check_vma=False)
```

```python
import functools

import jax
import jax.numpy as jnp
from jax import lax
from jax.experimental import pallas as pl
from jax.experimental.pallas import tpu as pltpu
from jax.sharding import PartitionSpec as P

HQ = 64
KVH = 8
DH = 128
LEN = 512
STEPS = 4
MESH = pl.DeviceIdType.MESH

rope_theta = 1000000.0
low_rank_scale = 0.5
epsilon = 1e-06

TOK = 128
WROWS = 64
PLANE = 2048
QKV = 1280
OUT = 1024
CW = 256
NC = QKV // CW
NO = OUT // CW


def coords():
    f = lax.axis_index("fsdp")
    t = lax.axis_index("tp")
    return f // 4, lax.rem(f // 2, 2), lax.rem(f, 2), t


def flip(v, bit):
    return 1 - v if bit else v


def xor_z(z, e):
    hi, lo = z // 2, lax.rem(z, 2)
    return flip(hi, e >> 1) * 2 + flip(lo, e & 1)


def xor_t(t, d):
    b2, b1, b0 = t // 4, lax.rem(t // 2, 2), lax.rem(t, 2)
    return flip(b2, (d >> 2) & 1) * 4 + flip(b1, (d >> 1) & 1) * 2 + flip(b0, d & 1)


def dev(z, xl, c, t):
    return ((z * 2 + xl) * 2 + c, t)


def remote(src, dst, ssem, rsem, device):
    return pltpu.make_async_remote_copy(
        src_ref=src, dst_ref=dst, send_sem=ssem, recv_sem=rsem, device_id=device, device_id_type=MESH
    )


def layer_kernel(
    a_ref, w_ref, o_ref, cos_ref, sin_ref, len_ref, k_ref, v_ref, out_ref,
    abuf, wbuf, acc, crecv, ostage, wo_ref, kbuf, vbuf, qbuf, knew, vnew, mixed, heads, hbuf, dsend, drecv,
    a_ss, a_rs, w1_ss, w1_rs, w2_ss, w2_rs, w3_ss, w3_rs, c_ss, c_rs,
    o1_ss, o1_rs, r1_ss, r1_rs, r2_ss, r2_rs, r3_ss, r3_rs,
    kv_s, h_ss, h_rs, d_ss, d_rs,
):
    z, xl, c, t = coords()
    xh = t // 4
    y = lax.rem(t, 4)
    xpart = dev(z, 1 - xl, c, t)
    xcross = dev(z, 1 - xl, c, y + 4 * (1 - xh))
    ring = (xpart, xcross)
    cpart = dev(z, xl, 1 - c, t)

    def plane_peer(d):
        return dev(z, flip(xl, d >> 2), c, xor_t(t, d))

    def z_peer(e):
        return dev(xor_z(z, e), xl, c, t)

    zd = t // 2
    half = lax.rem(t, 2)

    def parity(*bits):
        return lax.rem(sum(bits), 2)

    x_to = parity(xh, z, y // 2)
    here = (z == zd) & (xh == x_to)

    def h_target(d):
        return dev(zd, xl, c, x_to * 4 + xor_t(y, d))

    odd = parity(xh, z // 2, z)

    def h_source(i, h):
        return dev(2 * i + odd, xl, c, 2 * z + h)

    def d_target(i, j):
        return dev(2 * i + odd, xl, c, j * 4 + y)

    def d_source(p):
        return dev(p, xl, c, parity(z, p // 2, p) * 4 + y)

    cache = [
        pltpu.make_async_copy(k_ref, kbuf, kv_s.at[0]),
        pltpu.make_async_copy(v_ref, vbuf, kv_s.at[1]),
    ]

    barrier = pltpu.get_barrier_semaphore()
    peers = [plane_peer(d) for d in range(1, 8)] + [z_peer(e) for e in range(1, 4)] + [xpart, cpart, xcross]
    peers += [h_target(d) for d in range(4)] + [d_source(p) for p in range(4)]
    peers += [h_source(i, h) for i in range(2) for h in range(2)]
    peers += [d_target(i, j) for i in range(2) for j in range(2)]
    for p in peers:
        pl.semaphore_signal(barrier, inc=1, device_id=p, device_id_type=MESH)
    pl.semaphore_wait(barrier, len(peers))

    def a_copy(e):
        cols = pl.ds(pl.multiple_of(xor_z(z, e) * PLANE, PLANE), PLANE)
        if e == 0:
            return pltpu.make_async_copy(a_ref.at[:, cols], abuf.at[0], a_rs.at[0])
        return remote(a_ref.at[:, cols], abuf.at[e], a_ss.at[e], a_rs.at[e], z_peer(e))

    my_slot = (xl * 2 + c) * 8 + t

    def w1_copy(ch, d):
        td = xor_t(t, d)
        cols = pl.ds(pl.multiple_of(td * QKV + ch * CW, CW), CW)
        src = w_ref.at[:, cols]
        dst = wbuf.at[ch, my_slot]
        if d == 0:
            return pltpu.make_async_copy(src, dst, w1_rs.at[ch, 0])
        return remote(src, dst, w1_ss.at[ch, d], w1_rs.at[ch, d], plane_peer(d))

    def o_slot(source, d):
        lo = xl if source in (0, 3) else 1 - xl
        hi = xh if source in (0, 1) else 1 - xh
        return lo, hi, xor_t(y, d)

    def o_rows(source, d, core):
        lo, hi, row = o_slot(source, d)
        return wo_ref.at[(lo * 2 + core) * 8 + hi * 4 + row]

    def o_mine(d):
        return o_ref.at[:, pl.ds(pl.multiple_of(xor_t(y, d) * 2 * OUT, 2 * OUT), 2 * OUT)]

    def o1_copy(d):
        if d == 0:
            return pltpu.make_async_copy(o_mine(0), ostage, o1_rs.at[0])
        return remote(o_mine(d), wo_ref.at[my_slot], o1_ss.at[d], o1_rs.at[d], dev(z, xl, c, xh * 4 + xor_t(y, d)))

    def o1_wait(d):
        ref = o_rows(0, d, c)
        remote(ref, ref, o1_ss.at[d], o1_rs.at[d], xpart).wait_recv()

    def o_keep():
        return pltpu.make_async_copy(ostage, wo_ref.at[my_slot], o1_ss.at[0])

    def r1_copy(n, d):
        src = ostage if d == 0 else o_rows(0, d, c)
        return remote(src, o_rows(0, d, c), r1_ss.at[n, d], r1_rs.at[n, d], ring[n])

    def r1_wait(n, d):
        ref = o_rows(1 + n, d, c)
        remote(ref, ref, r1_ss.at[n, d], r1_rs.at[n, d], ring[n]).wait_recv()

    def r2_copy(d):
        n = 0 if d == 2 else 1
        ref = o_rows(2 - n, d, c)
        return remote(ref, ref, r2_ss.at[d], r2_rs.at[d], ring[n])

    def r2_wait(d):
        ref = o_rows(3, d, c)
        remote(ref, ref, r2_ss.at[d], r2_rs.at[d], xpart).wait_recv()

    def r3_copy(source, d):
        ref = o_rows(source, d, c)
        src = ostage if (source, d) == (0, 0) else ref
        return remote(src, ref, r3_ss.at[source, d], r3_rs.at[source, d], cpart)

    def r3_wait(source, d):
        ref = o_rows(source, d, 1 - c)
        remote(ref, ref, r3_ss.at[source, d], r3_rs.at[source, d], cpart).wait_recv()

    def group_base(g, core):
        lo = xl if g in (0, 3) else 1 - xl
        hi = xh if g in (0, 2) else 1 - xh
        return (lo * 2 + core) * 8 + hi * 4

    def w2_copy(k, g):
        ref = wbuf.at[k, pl.ds(group_base(g, c), 4)]
        return remote(ref, ref, w2_ss.at[k, g], w2_rs.at[k, g], xpart)

    def w2_wait(k, g):
        ref = wbuf.at[k, pl.ds(group_base(g + 2, c), 4)]
        remote(ref, ref, w2_ss.at[k, g], w2_rs.at[k, g], xpart).wait_recv()

    def w3_copy(k, g):
        ref = wbuf.at[k, pl.ds(group_base(g, c), 4)]
        return remote(ref, ref, w3_ss.at[k, g], w3_rs.at[k, g], cpart)

    def w3_wait(k, g):
        ref = wbuf.at[k, pl.ds(group_base(g, 1 - c), 4)]
        remote(ref, ref, w3_ss.at[k, g], w3_rs.at[k, g], cpart).wait_recv()

    def c_copy(ch, e):
        return remote(acc.at[ch, e], crecv.at[ch, e - 1], c_ss.at[ch, e], c_rs.at[ch, e], z_peer(e))

    def start_w1(ch, carry):
        for d in range(8):
            w1_copy(ch, d).start()
        return carry

    start_w1(0, 0)
    for e in (1, 3, 2, 0):
        a_copy(e).start()
    o1_copy(0).start()
    for copy in cache:
        copy.start()
    lax.fori_loop(1, NC, start_w1, 0)
    for d in (1, 3, 2):
        o1_copy(d).start()

    def relay(k):
        for g in range(2):
            for d in range(g * 4, g * 4 + 4):
                source_slot = (flip(xl, d >> 2) * 2 + c) * 8 + xor_t(t, d)
                if d == 0:
                    w1_copy(k, 0).wait()
                else:
                    ref = wbuf.at[k, source_slot]
                    remote(ref, ref, w1_ss.at[k, d], w1_rs.at[k, d], plane_peer(d)).wait_recv()
            w2_copy(k, g).start()
            w3_copy(k, g).start()

    def share(k):
        for g in range(2):
            w2_wait(k, g)
            w3_copy(k, g + 2).start()

    def multiply(ch):
        for g in range(4):
            w3_wait(ch, g)
        rows = abuf[...].reshape(4 * TOK, PLANE)
        part = jnp.dot(rows, wbuf[ch].reshape(PLANE, CW), preferred_element_type=jnp.float32)
        acc[ch] = part.reshape(4, TOK, CW)
        for e in (1, 3, 2):
            c_copy(ch, e).start()

    relay(0)
    o1_copy(0).wait()
    r1_copy(1, 0).start()
    r3_copy(0, 0).start()
    o_keep().start()
    for ch in range(3):
        relay(ch + 1)
        share(ch)
    r1_copy(0, 0).start()
    relay(4)
    share(3)
    a_copy(0).wait()
    for e in (1, 3, 2):
        a_copy(e).wait_recv()
    multiply(0)
    multiply(1)

    def spread(d):
        o1_wait(d)
        r1_copy(1, d).start()
        r1_copy(0, d).start()
        r3_copy(0, d).start()

    spread(1)
    multiply(2)
    spread(3)
    multiply(3)
    spread(2)
    share(4)
    multiply(4)

    def forward(d):
        n = 0 if d == 2 else 1
        r1_wait(1 - n, d)
        r2_copy(d).start()
        r3_copy(2 - n, d).start()

    def keep(d):
        n = 1 if d == 2 else 0
        r1_wait(1 - n, d)
        r3_copy(2 - n, d).start()

    forward(0)
    keep(0)
    keep(1)
    keep(3)
    forward(2)
    forward(1)
    forward(3)
    keep(2)
    def rope(values):
        return values * cos_ref[...] + pltpu.roll(values, DH // 2, axis=1) * sin_ref[...]

    for ch in range(NC):
        for e in range(1, 4):
            c_copy(ch, e).wait_recv()
        part = acc[ch, 0] + crecv[ch, 0] + crecv[ch, 1] + crecv[ch, 2]
        first, second = part[:, :DH], part[:, DH:]
        if ch < NC - 1:
            qbuf[2 * ch] = rope(first).astype(jnp.bfloat16).astype(jnp.float32)
            qbuf[2 * ch + 1] = rope(second).astype(jnp.bfloat16).astype(jnp.float32)
        else:
            knew[...] = rope(first).astype(jnp.bfloat16)
            vnew[...] = second.astype(jnp.bfloat16)
    for copy in cache:
        copy.wait()

    score_scale = DH ** (-0.5)
    contract_last = (((1,), (1,)), ((), ()))

    def attend_pair(p):
        tokens = pl.ds(pl.multiple_of(p * 8, 8), 8)
        queries = qbuf[:, tokens, :].reshape(64, DH).astype(jnp.bfloat16)
        keys = kbuf[pl.ds(2 * p, 2)].reshape(2 * LEN, DH)
        values = vbuf[pl.ds(2 * p, 2)].reshape(2 * LEN, DH)
        token = lax.rem(lax.broadcasted_iota(jnp.int32, (64, 1), 0), 8)
        second = token >= STEPS
        low = jnp.where(second, LEN, 0)
        high = low + jnp.where(second, len_ref[2 * p + 1], len_ref[2 * p])
        slot = lax.broadcasted_iota(jnp.int32, (64, 2 * LEN), 1)
        old = lax.dot_general(queries, keys, contract_last, preferred_element_type=jnp.float32) * score_scale
        old = jnp.where((slot >= low) & (slot < high), old, -1e30)
        column = lax.broadcasted_iota(jnp.int32, (64, TOK), 1)
        last = p * 8 + token
        begin = p * 8 + jnp.where(second, STEPS, 0)
        new = lax.dot_general(queries, knew[...], contract_last, preferred_element_type=jnp.float32) * score_scale
        new = jnp.where((column >= begin) & (column <= last), new, -1e30)
        highest = jnp.maximum(jnp.max(old, -1, keepdims=True), jnp.max(new, -1, keepdims=True))
        old_exp = jnp.exp(old - highest)
        new_exp = jnp.exp(new - highest)
        inverse = 1.0 / (jnp.sum(old_exp, -1, keepdims=True) + jnp.sum(new_exp, -1, keepdims=True))
        old_weights = (old_exp * inverse).astype(jnp.bfloat16)
        new_weights = (new_exp * inverse).astype(jnp.bfloat16)
        mixture = jnp.dot(old_weights, values, preferred_element_type=jnp.float32)
        mixture = mixture + jnp.dot(new_weights, vnew[...], preferred_element_type=jnp.float32)
        for g in range(8):
            mixed[tokens, g * DH : (g + 1) * DH] = mixture[g * 8 : (g + 1) * 8]

    QT = TOK // 4

    def h_rows(qt):
        return heads.at[pl.ds(pl.multiple_of(qt * QT, QT), QT)]

    def h_slot(qt):
        return hbuf.at[z // 2, pl.ds(pl.multiple_of(qt * QT, QT), QT), pl.ds(pl.multiple_of(half * OUT, OUT), OUT)]

    def h_send(qt, d):
        return remote(h_rows(qt), h_slot(qt), h_ss.at[qt, d], h_rs.at[z // 2, half, qt], h_target(d))

    def h_local(qt):
        return pltpu.make_async_copy(h_rows(qt), h_slot(qt), h_rs.at[z // 2, half, qt])

    def quarter(qt, carry):
        for n in range(4):
            attend_pair(qt * 4 + n)
        rows = pl.ds(pl.multiple_of(qt * QT, QT), QT)
        heads[rows] = mixed[rows].astype(jnp.bfloat16)
        for d in (2, 1, 3):
            h_send(qt, d).start()

        @pl.when(here)
        def _():
            h_local(qt).start()

        @pl.when(jnp.logical_not(here))
        def _():
            h_send(qt, 0).start()

        return carry

    lax.fori_loop(0, 4, quarter, 0)

    for d in (0, 1, 3, 2):
        r2_wait(d)
        r3_copy(3, d).start()
    for source in range(4):
        for d in range(4):
            r3_wait(source, d)
    o_keep().wait()

    for i in range(2):
        for h in range(2):
            for qt in range(4):
                ref = hbuf.at[i, pl.ds(qt * QT, QT), pl.ds(h * OUT, OUT)]
                pltpu.make_async_copy(ref, ref, h_rs.at[i, h, qt]).wait()

    def mine(i, j):
        return (2 * i + odd == z) & (xh == j)

    def d_copy(n, j, i):
        return remote(
            dsend.at[j, n, i], drecv.at[n, z], d_ss.at[j, n, i], d_rs.at[n, z], d_target(i, j)
        )

    def d_local(n, j, i):
        return pltpu.make_async_copy(dsend.at[j, n, i], drecv.at[n, z], d_rs.at[n, z])

    for n in range(NO):
        for j in range(2):
            lo = j * OUT + n * CW
            w = wo_ref[:, :, lo : lo + CW].reshape(PLANE, CW)
            part = jnp.dot(hbuf[...].reshape(2 * TOK, PLANE), w, preferred_element_type=jnp.float32)
            dsend[j, n] = part.astype(jnp.bfloat16).reshape(2, TOK, CW)
            for i in range(2):

                @pl.when(mine(i, j))
                def _():
                    d_local(n, j, i).start()

                @pl.when(jnp.logical_not(mine(i, j)))
                def _():
                    d_copy(n, j, i).start()

    for n in range(NO):
        total = None
        for p in range(4):
            ref = drecv.at[n, p]
            pltpu.make_async_copy(ref, ref, d_rs.at[n, p]).wait()
            part = drecv[n, p].astype(jnp.float32)
            total = part if total is None else total + part
        out_ref[:, :, n * CW : (n + 1) * CW] = total.reshape(TOK // STEPS, STEPS, CW).astype(jnp.bfloat16)

    def drain_heads(qt, carry):
        for d in range(1, 4):
            h_send(qt, d).wait_send()

        @pl.when(jnp.logical_not(here))
        def _():
            h_send(qt, 0).wait_send()

        return carry

    lax.fori_loop(0, 4, drain_heads, 0)
    for n in range(NO):
        for j in range(2):
            for i in range(2):

                @pl.when(jnp.logical_not(mine(i, j)))
                def _():
                    d_copy(n, j, i).wait_send()

    for e in range(1, 4):
        a_copy(e).wait_send()

    def drain(ch, carry):
        for d in range(1, 8):
            w1_copy(ch, d).wait_send()
        for g in range(2):
            w2_copy(ch, g).wait_send()
        for g in range(4):
            w3_copy(ch, g).wait_send()
        for e in range(1, 4):
            c_copy(ch, e).wait_send()
        return carry

    lax.fori_loop(0, NC, drain, 0)
    for d in range(1, 4):
        o1_copy(d).wait_send()
    for d in range(4):
        r1_copy(0, d).wait_send()
        r1_copy(1, d).wait_send()
        r2_copy(d).wait_send()
        for source in range(4):
            r3_copy(source, d).wait_send()


VM = pl.BlockSpec(memory_space=pltpu.VMEM)
ANY = pl.BlockSpec(memory_space=pl.ANY)
DMA = pltpu.SemaphoreType.DMA


def run_layer(normed, joined, merged_output, cosine, sine, lengths, keys, values):
    return pl.pallas_call(
        layer_kernel,
        out_shape=jax.ShapeDtypeStruct((TOK // STEPS, STEPS, OUT), jnp.bfloat16),
        in_specs=[ANY, ANY, ANY, VM, VM, pl.BlockSpec(memory_space=pltpu.SMEM), ANY, ANY],
        out_specs=VM,
        scratch_shapes=[
            pltpu.VMEM((4, TOK, PLANE), jnp.bfloat16),
            pltpu.VMEM((NC, 32, WROWS, CW), jnp.bfloat16),
            pltpu.VMEM((NC, 4, TOK, CW), jnp.float32),
            pltpu.VMEM((NC, 3, TOK, CW), jnp.float32),
            pltpu.VMEM((WROWS, 2 * OUT), jnp.bfloat16),
            pltpu.VMEM((32, WROWS, 2 * OUT), jnp.bfloat16),
            pltpu.VMEM(keys.shape, jnp.bfloat16),
            pltpu.VMEM(values.shape, jnp.bfloat16),
            pltpu.VMEM((8, TOK, DH), jnp.float32),
            pltpu.VMEM((TOK, DH), jnp.bfloat16),
            pltpu.VMEM((TOK, DH), jnp.bfloat16),
            pltpu.VMEM((TOK, OUT), jnp.float32),
            pltpu.VMEM((TOK, OUT), jnp.bfloat16),
            pltpu.VMEM((2, TOK, PLANE), jnp.bfloat16),
            pltpu.VMEM((2, NO, 2, TOK, CW), jnp.bfloat16),
            pltpu.VMEM((NO, 4, TOK, CW), jnp.bfloat16),
            DMA((4,)), DMA((4,)),
            DMA((NC, 8)), DMA((NC, 8)),
            DMA((NC, 2)), DMA((NC, 2)),
            DMA((NC, 4)), DMA((NC, 4)),
            DMA((NC, 4)), DMA((NC, 4)),
            DMA((4,)), DMA((4,)),
            DMA((2, 4)), DMA((2, 4)),
            DMA((4,)), DMA((4,)),
            DMA((4, 4)), DMA((4, 4)),
            DMA((2,)),
            DMA((4, 4)), DMA((2, 2, 4)),
            DMA((2, NO, 2)), DMA((NO, 4)),
        ],
        compiler_params=pltpu.CompilerParams(collective_id=0, has_side_effects=True, vmem_limit_bytes=62 << 20),
        name="layer",
    )(normed, joined, merged_output, cosine, sine, lengths, keys, values)


def prepare_kernel(
    slot_ref, gain_ref, states_ref, q_ref, k_ref, v_ref, o_ref,
    qd_ref, kd_ref, vd_ref, od_ref, qu_ref, ku_ref, vu_ref, ou_ref,
    normed_ref, joined_ref, merged_ref,
):
    def merge(base, down, up):
        delta = jnp.dot(down[0], up[0], preferred_element_type=jnp.float32)
        return (base[...].astype(jnp.float32) + low_rank_scale * delta).astype(jnp.bfloat16)

    head_cols = q_ref.shape[1]
    kv_cols = k_ref.shape[1]
    joined_ref[:, :head_cols] = merge(q_ref, qd_ref, qu_ref)
    joined_ref[:, head_cols : head_cols + kv_cols] = merge(k_ref, kd_ref, ku_ref)
    joined_ref[:, head_cols + kv_cols :] = merge(v_ref, vd_ref, vu_ref)
    merged_ref[...] = merge(o_ref, od_ref, ou_ref)
    widened = states_ref[...].astype(jnp.float32)
    squared_average = jnp.mean(widened * widened, axis=-1, keepdims=True)
    normed = widened * lax.rsqrt(squared_average + epsilon) * gain_ref[...].reshape(1, 1, -1)
    normed_ref[...] = normed.reshape(normed_ref.shape).astype(jnp.bfloat16)


def prepare(slot, gain, states, bases, downs, ups):
    steps = 8
    seqs, decode, width = states.shape
    block = seqs // steps

    def cols(array):
        return pl.BlockSpec((array.shape[0], array.shape[1] // steps), lambda i, s: (0, i))

    def down(array):
        return pl.BlockSpec((1, *array.shape[1:]), lambda i, s: (s[0], 0, 0))

    def up(array):
        return pl.BlockSpec((1, array.shape[1], array.shape[2] // steps), lambda i, s: (s[0], 0, i))

    return pl.pallas_call(
        prepare_kernel,
        out_shape=(
            jax.ShapeDtypeStruct((seqs * decode, width), jnp.bfloat16),
            jax.ShapeDtypeStruct((WROWS, QKV * steps), jnp.bfloat16),
            jax.ShapeDtypeStruct((WROWS, OUT * steps), jnp.bfloat16),
        ),
        grid_spec=pltpu.PrefetchScalarGridSpec(
            num_scalar_prefetch=1,
            grid=(steps,),
            in_specs=[
                pl.BlockSpec((1, width), lambda i, s: (0, 0)),
                pl.BlockSpec((block, decode, width), lambda i, s: (i, 0, 0)),
                *[cols(b) for b in bases],
                *[down(d) for d in downs],
                *[up(u) for u in ups],
            ],
            out_specs=(
                pl.BlockSpec((block * decode, width), lambda i, s: (i, 0)),
                pl.BlockSpec((WROWS, QKV), lambda i, s: (0, i)),
                pl.BlockSpec((WROWS, OUT), lambda i, s: (0, lax.rem(i, 4) * 2 + i // 4)),
            ),
        ),
        name="prepare",
    )(slot, gain.reshape(1, -1), states, *bases, *downs, *ups)


def rope_tables(positions):
    half_dim = DH // 2
    frequency = rope_theta ** (-2.0 * jnp.arange(half_dim, dtype=jnp.float32) / DH)
    rotation_phases = positions[:, None] * frequency[None, :]
    cosine, sine = jnp.cos(rotation_phases), jnp.sin(rotation_phases)
    return jnp.concatenate((cosine, cosine), -1), jnp.concatenate((-sine, sine), -1)


def local(
    states,
    norm_gain,
    query_base,
    key_base,
    value_base,
    output_base,
    query_down,
    query_up,
    key_down,
    key_up,
    value_down,
    value_up,
    output_down,
    output_up,
    adapter_layer,
    kv_lengths,
    cache_keys,
    cache_values,
):
    seq_count, step_count, _ = states.shape
    normed, joined, merged_output = prepare(
        adapter_layer,
        norm_gain,
        states,
        (query_base, key_base, value_base, output_base),
        (query_down, key_down, value_down, output_down),
        (query_up, key_up, value_up, output_up),
    )
    positions = (
        kv_lengths.astype(jnp.float32)[:, None] + jnp.arange(step_count, dtype=jnp.float32)[None, :]
    )
    cosine, sine = rope_tables(positions.reshape(-1))
    keys = cache_keys.reshape(seq_count, -1, DH)
    values = cache_values.reshape(seq_count, -1, DH)
    return run_layer(normed, joined, merged_output, cosine, sine, kv_lengths, keys, values)


def solution(mesh):
    in_specs = (
        P("fsdp", None, None),
        P(),
        P(("fsdp", "tp"), None),
        P(("fsdp", "tp"), None),
        P(("fsdp", "tp"), None),
        P(("fsdp", "tp"), None),
        P(None, ("fsdp", "tp"), None),
        P(),
        P(None, ("fsdp", "tp"), None),
        P(),
        P(None, ("fsdp", "tp"), None),
        P(),
        P(None, ("fsdp", "tp"), None),
        P(),
        P(),
        P("fsdp"),
        P("fsdp", None, "tp", None),
        P("fsdp", None, "tp", None),
    )
    out_specs = P("fsdp", None, "tp")
    return jax.shard_map(local, mesh=mesh, in_specs=in_specs, out_specs=out_specs, check_vma=False)
```

```python
import functools

import jax
import jax.numpy as jnp
from jax import lax
from jax.experimental import pallas as pl
from jax.experimental.pallas import tpu as pltpu
from jax.sharding import PartitionSpec as P

HQ = 64
KVH = 8
DH = 128
LEN = 512
STEPS = 4
MESH = pl.DeviceIdType.MESH

rope_theta = 1000000.0
low_rank_scale = 0.5
epsilon = 1e-06

TOK = 128
WROWS = 64
PLANE = 2048
QKV = 1280
OUT = 1024
CW = 256
NC = QKV // CW
NO = OUT // CW


def coords():
    f = lax.axis_index("fsdp")
    t = lax.axis_index("tp")
    return f // 4, lax.rem(f // 2, 2), lax.rem(f, 2), t


def flip(v, bit):
    return 1 - v if bit else v


def xor_z(z, e):
    hi, lo = z // 2, lax.rem(z, 2)
    return flip(hi, e >> 1) * 2 + flip(lo, e & 1)


def xor_t(t, d):
    b2, b1, b0 = t // 4, lax.rem(t // 2, 2), lax.rem(t, 2)
    return flip(b2, (d >> 2) & 1) * 4 + flip(b1, (d >> 1) & 1) * 2 + flip(b0, d & 1)


def dev(z, xl, c, t):
    return ((z * 2 + xl) * 2 + c, t)


def remote(src, dst, ssem, rsem, device):
    return pltpu.make_async_remote_copy(
        src_ref=src, dst_ref=dst, send_sem=ssem, recv_sem=rsem, device_id=device, device_id_type=MESH
    )


def layer_kernel(
    a_ref, w_ref, o_ref, cos_ref, sin_ref, len_ref, k_ref, v_ref, out_ref,
    abuf, wbuf, acc, crecv, ostage, wo_ref, kbuf, vbuf, qbuf, knew, vnew, mixed, heads, hbuf, dsend, drecv,
    a_ss, a_rs, w1_ss, w1_rs, w2_ss, w2_rs, w3_ss, w3_rs, c_ss, c_rs,
    o1_ss, o1_rs, r1_ss, r1_rs, r2_ss, r2_rs, r3_ss, r3_rs,
    kv_s, h_ss, h_rs, d_ss, d_rs,
):
    z, xl, c, t = coords()
    xh = t // 4
    y = lax.rem(t, 4)
    xpart = dev(z, 1 - xl, c, t)
    ring = (dev(z, xl, c, xor_t(t, 1)), dev(z, xl, c, xor_t(t, 3)))

    def x_peer(d):
        return flip(xl, d & 1), flip(xh, d >> 1)
    cpart = dev(z, xl, 1 - c, t)

    def plane_peer(d):
        return dev(z, flip(xl, d >> 2), c, xor_t(t, d))

    def z_peer(e):
        return dev(xor_z(z, e), xl, c, t)

    zd = t // 2
    half = lax.rem(t, 2)

    y_to = lax.rem(z + 2 * (y // 2) + xh, 4)
    here = (z == zd) & (y == y_to)

    def h_target(d):
        lo, hi = x_peer(d)
        return dev(zd, lo, c, hi * 4 + y_to)

    z_rows = lax.rem(y + 8 - 2 * lax.rem(z, 2) - z // 2, 4)

    def h_source(i, h):
        return dev(z_rows, i, c, 2 * z + h)

    def d_target(i, j):
        return dev(z_rows, i, c, xh * 4 + 2 * xl + j)

    def d_source(p):
        return dev(p, y // 2, c, xh * 4 + lax.rem(z + 2 * (p % 2) + p // 2, 4))

    cache = [
        pltpu.make_async_copy(k_ref, kbuf, kv_s.at[0]),
        pltpu.make_async_copy(v_ref, vbuf, kv_s.at[1]),
    ]

    barrier = pltpu.get_barrier_semaphore()
    peers = [plane_peer(d) for d in range(1, 8)] + [z_peer(e) for e in range(1, 4)] + [xpart, cpart, dev(z, xl, c, xor_t(t, 4))]
    peers += [h_target(d) for d in range(4)] + [d_source(p) for p in range(4)]
    peers += [h_source(i, h) for i in range(2) for h in range(2)]
    peers += [d_target(i, j) for i in range(2) for j in range(2)]
    for p in peers:
        pl.semaphore_signal(barrier, inc=1, device_id=p, device_id_type=MESH)
    pl.semaphore_wait(barrier, len(peers))

    def a_copy(e):
        cols = pl.ds(pl.multiple_of(xor_z(z, e) * PLANE, PLANE), PLANE)
        if e == 0:
            return pltpu.make_async_copy(a_ref.at[:, cols], abuf.at[0], a_rs.at[0])
        return remote(a_ref.at[:, cols], abuf.at[e], a_ss.at[e], a_rs.at[e], z_peer(e))

    my_slot = (xl * 2 + c) * 8 + t

    def w1_copy(ch, d):
        td = xor_t(t, d)
        cols = pl.ds(pl.multiple_of(td * QKV + ch * CW, CW), CW)
        src = w_ref.at[:, cols]
        dst = wbuf.at[ch, my_slot]
        if d == 0:
            return pltpu.make_async_copy(src, dst, w1_rs.at[ch, 0])
        return remote(src, dst, w1_ss.at[ch, d], w1_rs.at[ch, d], plane_peer(d))

    def o_rows(source, d, core):
        lo, hi = x_peer(d)
        return wo_ref.at[(lo * 2 + core) * 8 + hi * 4 + xor_t(y, (0, 1, 3, 2)[source])]

    def o_mine(d):
        lo, hi = x_peer(d)
        return o_ref.at[:, pl.ds(pl.multiple_of((hi * 2 + lo) * 2 * OUT, 2 * OUT), 2 * OUT)]

    def o1_copy(d):
        if d == 0:
            return pltpu.make_async_copy(o_mine(0), ostage, o1_rs.at[0])
        lo, hi = x_peer(d)
        return remote(o_mine(d), wo_ref.at[my_slot], o1_ss.at[d], o1_rs.at[d], dev(z, lo, c, hi * 4 + y))

    def o1_wait(d):
        ref = o_rows(0, d, c)
        remote(ref, ref, o1_ss.at[d], o1_rs.at[d], xpart).wait_recv()

    def o_keep():
        return pltpu.make_async_copy(ostage, wo_ref.at[my_slot], o1_ss.at[0])

    def r1_copy(n, d):
        src = ostage if d == 0 else o_rows(0, d, c)
        return remote(src, o_rows(0, d, c), r1_ss.at[n, d], r1_rs.at[n, d], ring[n])

    def r1_wait(n, d):
        ref = o_rows(1 + n, d, c)
        remote(ref, ref, r1_ss.at[n, d], r1_rs.at[n, d], ring[n]).wait_recv()

    def r2_copy(d):
        n = d >> 1
        ref = o_rows(2 - n, d, c)
        return remote(ref, ref, r2_ss.at[d], r2_rs.at[d], ring[n])

    def r2_wait(d):
        ref = o_rows(3, d, c)
        remote(ref, ref, r2_ss.at[d], r2_rs.at[d], xpart).wait_recv()

    def r3_copy(source, d):
        ref = o_rows(source, d, c)
        src = ostage if (source, d) == (0, 0) else ref
        return remote(src, ref, r3_ss.at[source, d], r3_rs.at[source, d], cpart)

    def r3_wait(source, d):
        ref = o_rows(source, d, 1 - c)
        remote(ref, ref, r3_ss.at[source, d], r3_rs.at[source, d], cpart).wait_recv()

    def group_base(g, core):
        lo = xl if g in (0, 3) else 1 - xl
        hi = xh if g in (0, 2) else 1 - xh
        return (lo * 2 + core) * 8 + hi * 4

    def w2_copy(k, g):
        ref = wbuf.at[k, pl.ds(group_base(g, c), 4)]
        return remote(ref, ref, w2_ss.at[k, g], w2_rs.at[k, g], xpart)

    def w2_wait(k, g):
        ref = wbuf.at[k, pl.ds(group_base(g + 2, c), 4)]
        remote(ref, ref, w2_ss.at[k, g], w2_rs.at[k, g], xpart).wait_recv()

    def w3_copy(k, g):
        ref = wbuf.at[k, pl.ds(group_base(g, c), 4)]
        return remote(ref, ref, w3_ss.at[k, g], w3_rs.at[k, g], cpart)

    def w3_wait(k, g):
        ref = wbuf.at[k, pl.ds(group_base(g, 1 - c), 4)]
        remote(ref, ref, w3_ss.at[k, g], w3_rs.at[k, g], cpart).wait_recv()

    def c_copy(ch, e):
        return remote(acc.at[ch, e], crecv.at[ch, e - 1], c_ss.at[ch, e], c_rs.at[ch, e], z_peer(e))

    def start_w1(ch, carry):
        for d in range(8):
            w1_copy(ch, d).start()
        return carry

    start_w1(0, 0)
    for e in (1, 3, 2, 0):
        a_copy(e).start()
    o1_copy(0).start()
    for copy in cache:
        copy.start()
    lax.fori_loop(1, NC, start_w1, 0)
    for d in (1, 3, 2):
        o1_copy(d).start()

    def relay(k):
        for g in range(2):
            for d in range(g * 4, g * 4 + 4):
                source_slot = (flip(xl, d >> 2) * 2 + c) * 8 + xor_t(t, d)
                if d == 0:
                    w1_copy(k, 0).wait()
                else:
                    ref = wbuf.at[k, source_slot]
                    remote(ref, ref, w1_ss.at[k, d], w1_rs.at[k, d], plane_peer(d)).wait_recv()
            w2_copy(k, g).start()
            w3_copy(k, g).start()

    def share(k):
        for g in range(2):
            w2_wait(k, g)
            w3_copy(k, g + 2).start()

    def multiply(ch):
        for g in range(4):
            w3_wait(ch, g)
        rows = abuf[...].reshape(4 * TOK, PLANE)
        part = jnp.dot(rows, wbuf[ch].reshape(PLANE, CW), preferred_element_type=jnp.float32)
        acc[ch] = part.reshape(4, TOK, CW)
        for e in (1, 3, 2):
            c_copy(ch, e).start()

    def spread(d):
        o1_wait(d)
        r1_copy(0, d).start()
        r1_copy(1, d).start()
        r3_copy(0, d).start()

    def forward(d):
        n = d >> 1
        r1_wait(1 - n, d)
        r2_copy(d).start()
        r3_copy(2 - n, d).start()

    def keep(d):
        n = 1 - (d >> 1)
        r1_wait(1 - n, d)
        r3_copy(2 - n, d).start()

    relay(0)
    o1_copy(0).wait()
    r1_copy(0, 0).start()
    r1_copy(1, 0).start()
    r3_copy(0, 0).start()
    o_keep().start()
    relay(1)
    share(0)
    spread(1)
    relay(2)
    share(1)
    spread(3)
    relay(3)
    share(2)
    spread(2)
    relay(4)
    a_copy(0).wait()
    for e in (1, 3, 2):
        a_copy(e).wait_recv()
    multiply(0)
    share(3)
    multiply(1)
    forward(0)
    keep(0)
    multiply(2)
    forward(1)
    keep(1)
    multiply(3)
    share(4)
    multiply(4)
    forward(3)
    keep(3)
    forward(2)
    keep(2)

    def rope(values):
        return values * cos_ref[...] + pltpu.roll(values, DH // 2, axis=1) * sin_ref[...]

    for ch in range(NC):
        for e in range(1, 4):
            c_copy(ch, e).wait_recv()
        part = acc[ch, 0] + crecv[ch, 0] + crecv[ch, 1] + crecv[ch, 2]
        first, second = part[:, :DH], part[:, DH:]
        if ch < NC - 1:
            qbuf[2 * ch] = rope(first).astype(jnp.bfloat16).astype(jnp.float32)
            qbuf[2 * ch + 1] = rope(second).astype(jnp.bfloat16).astype(jnp.float32)
        else:
            knew[...] = rope(first).astype(jnp.bfloat16)
            vnew[...] = second.astype(jnp.bfloat16)
    for copy in cache:
        copy.wait()

    score_scale = DH ** (-0.5)
    contract_last = (((1,), (1,)), ((), ()))

    def attend_pair(p):
        tokens = pl.ds(pl.multiple_of(p * 8, 8), 8)
        queries = qbuf[:, tokens, :].reshape(64, DH).astype(jnp.bfloat16)
        keys = kbuf[pl.ds(2 * p, 2)].reshape(2 * LEN, DH)
        values = vbuf[pl.ds(2 * p, 2)].reshape(2 * LEN, DH)
        token = lax.rem(lax.broadcasted_iota(jnp.int32, (64, 1), 0), 8)
        second = token >= STEPS
        low = jnp.where(second, LEN, 0)
        high = low + jnp.where(second, len_ref[2 * p + 1], len_ref[2 * p])
        slot = lax.broadcasted_iota(jnp.int32, (64, 2 * LEN), 1)
        old = lax.dot_general(queries, keys, contract_last, preferred_element_type=jnp.float32) * score_scale
        old = jnp.where((slot >= low) & (slot < high), old, -1e30)
        column = lax.broadcasted_iota(jnp.int32, (64, TOK), 1)
        last = p * 8 + token
        begin = p * 8 + jnp.where(second, STEPS, 0)
        new = lax.dot_general(queries, knew[...], contract_last, preferred_element_type=jnp.float32) * score_scale
        new = jnp.where((column >= begin) & (column <= last), new, -1e30)
        highest = jnp.maximum(jnp.max(old, -1, keepdims=True), jnp.max(new, -1, keepdims=True))
        old_exp = jnp.exp(old - highest)
        new_exp = jnp.exp(new - highest)
        inverse = 1.0 / (jnp.sum(old_exp, -1, keepdims=True) + jnp.sum(new_exp, -1, keepdims=True))
        old_weights = (old_exp * inverse).astype(jnp.bfloat16)
        new_weights = (new_exp * inverse).astype(jnp.bfloat16)
        mixture = jnp.dot(old_weights, values, preferred_element_type=jnp.float32)
        mixture = mixture + jnp.dot(new_weights, vnew[...], preferred_element_type=jnp.float32)
        for g in range(8):
            mixed[tokens, g * DH : (g + 1) * DH] = mixture[g * 8 : (g + 1) * 8]

    QT = TOK // 4

    def h_rows(qt):
        return heads.at[pl.ds(pl.multiple_of(qt * QT, QT), QT)]

    def h_slot(qt):
        return hbuf.at[xl, pl.ds(pl.multiple_of(qt * QT, QT), QT), pl.ds(pl.multiple_of(half * OUT, OUT), OUT)]

    def h_send(qt, d):
        return remote(h_rows(qt), h_slot(qt), h_ss.at[qt, d], h_rs.at[xl, half, qt], h_target(d))

    def h_local(qt):
        return pltpu.make_async_copy(h_rows(qt), h_slot(qt), h_rs.at[xl, half, qt])

    def quarter(qt, carry):
        for n in range(4):
            attend_pair(qt * 4 + n)
        rows = pl.ds(pl.multiple_of(qt * QT, QT), QT)
        heads[rows] = mixed[rows].astype(jnp.bfloat16)
        for d in (2, 1, 3):
            h_send(qt, d).start()

        @pl.when(here)
        def _():
            h_local(qt).start()

        @pl.when(jnp.logical_not(here))
        def _():
            h_send(qt, 0).start()

        return carry

    lax.fori_loop(0, 4, quarter, 0)

    for d in (0, 1, 3, 2):
        r2_wait(d)
        r3_copy(3, d).start()
    for source in range(4):
        for d in range(4):
            r3_wait(source, d)
    o_keep().wait()

    for i in range(2):
        for h in range(2):
            for qt in range(4):
                ref = hbuf.at[i, pl.ds(qt * QT, QT), pl.ds(h * OUT, OUT)]
                pltpu.make_async_copy(ref, ref, h_rs.at[i, h, qt]).wait()

    def mine(i, j):
        return (z_rows == z) & (xl == i) & (y == 2 * xl + j)

    def d_copy(n, j, i):
        return remote(
            dsend.at[j, n, i], drecv.at[n, z], d_ss.at[j, n, i], d_rs.at[n, z], d_target(i, j)
        )

    def d_local(n, j, i):
        return pltpu.make_async_copy(dsend.at[j, n, i], drecv.at[n, z], d_rs.at[n, z])

    for n in range(NO):
        for j in range(2):
            lo = j * OUT + n * CW
            w = wo_ref[:, :, lo : lo + CW].reshape(PLANE, CW)
            part = jnp.dot(hbuf[...].reshape(2 * TOK, PLANE), w, preferred_element_type=jnp.float32)
            dsend[j, n] = part.astype(jnp.bfloat16).reshape(2, TOK, CW)
            for i in range(2):

                @pl.when(mine(i, j))
                def _():
                    d_local(n, j, i).start()

                @pl.when(jnp.logical_not(mine(i, j)))
                def _():
                    d_copy(n, j, i).start()

    for n in range(NO):
        total = None
        for p in range(4):
            ref = drecv.at[n, p]
            pltpu.make_async_copy(ref, ref, d_rs.at[n, p]).wait()
            part = drecv[n, p].astype(jnp.float32)
            total = part if total is None else total + part
        out_ref[:, :, n * CW : (n + 1) * CW] = total.reshape(TOK // STEPS, STEPS, CW).astype(jnp.bfloat16)

    def drain_heads(qt, carry):
        for d in range(1, 4):
            h_send(qt, d).wait_send()

        @pl.when(jnp.logical_not(here))
        def _():
            h_send(qt, 0).wait_send()

        return carry

    lax.fori_loop(0, 4, drain_heads, 0)
    for n in range(NO):
        for j in range(2):
            for i in range(2):

                @pl.when(jnp.logical_not(mine(i, j)))
                def _():
                    d_copy(n, j, i).wait_send()

    for e in range(1, 4):
        a_copy(e).wait_send()

    def drain(ch, carry):
        for d in range(1, 8):
            w1_copy(ch, d).wait_send()
        for g in range(2):
            w2_copy(ch, g).wait_send()
        for g in range(4):
            w3_copy(ch, g).wait_send()
        for e in range(1, 4):
            c_copy(ch, e).wait_send()
        return carry

    lax.fori_loop(0, NC, drain, 0)
    for d in range(1, 4):
        o1_copy(d).wait_send()
    for d in range(4):
        r1_copy(0, d).wait_send()
        r1_copy(1, d).wait_send()
        r2_copy(d).wait_send()
        for source in range(4):
            r3_copy(source, d).wait_send()


VM = pl.BlockSpec(memory_space=pltpu.VMEM)
ANY = pl.BlockSpec(memory_space=pl.ANY)
DMA = pltpu.SemaphoreType.DMA


def run_layer(normed, joined, merged_output, cosine, sine, lengths, keys, values):
    return pl.pallas_call(
        layer_kernel,
        out_shape=jax.ShapeDtypeStruct((TOK // STEPS, STEPS, OUT), jnp.bfloat16),
        in_specs=[ANY, ANY, ANY, VM, VM, pl.BlockSpec(memory_space=pltpu.SMEM), ANY, ANY],
        out_specs=VM,
        scratch_shapes=[
            pltpu.VMEM((4, TOK, PLANE), jnp.bfloat16),
            pltpu.VMEM((NC, 32, WROWS, CW), jnp.bfloat16),
            pltpu.VMEM((NC, 4, TOK, CW), jnp.float32),
            pltpu.VMEM((NC, 3, TOK, CW), jnp.float32),
            pltpu.VMEM((WROWS, 2 * OUT), jnp.bfloat16),
            pltpu.VMEM((32, WROWS, 2 * OUT), jnp.bfloat16),
            pltpu.VMEM(keys.shape, jnp.bfloat16),
            pltpu.VMEM(values.shape, jnp.bfloat16),
            pltpu.VMEM((8, TOK, DH), jnp.float32),
            pltpu.VMEM((TOK, DH), jnp.bfloat16),
            pltpu.VMEM((TOK, DH), jnp.bfloat16),
            pltpu.VMEM((TOK, OUT), jnp.float32),
            pltpu.VMEM((TOK, OUT), jnp.bfloat16),
            pltpu.VMEM((2, TOK, PLANE), jnp.bfloat16),
            pltpu.VMEM((2, NO, 2, TOK, CW), jnp.bfloat16),
            pltpu.VMEM((NO, 4, TOK, CW), jnp.bfloat16),
            DMA((4,)), DMA((4,)),
            DMA((NC, 8)), DMA((NC, 8)),
            DMA((NC, 2)), DMA((NC, 2)),
            DMA((NC, 4)), DMA((NC, 4)),
            DMA((NC, 4)), DMA((NC, 4)),
            DMA((4,)), DMA((4,)),
            DMA((2, 4)), DMA((2, 4)),
            DMA((4,)), DMA((4,)),
            DMA((4, 4)), DMA((4, 4)),
            DMA((2,)),
            DMA((4, 4)), DMA((2, 2, 4)),
            DMA((2, NO, 2)), DMA((NO, 4)),
        ],
        compiler_params=pltpu.CompilerParams(collective_id=0, has_side_effects=True, vmem_limit_bytes=62 << 20),
        name="layer",
    )(normed, joined, merged_output, cosine, sine, lengths, keys, values)


def prepare_kernel(
    slot_ref, gain_ref, states_ref, q_ref, k_ref, v_ref, o_ref,
    qd_ref, kd_ref, vd_ref, od_ref, qu_ref, ku_ref, vu_ref, ou_ref,
    normed_ref, joined_ref, merged_ref,
):
    def merge(base, down, up):
        delta = jnp.dot(down[0], up[0], preferred_element_type=jnp.float32)
        return (base[...].astype(jnp.float32) + low_rank_scale * delta).astype(jnp.bfloat16)

    q, k, v = merge(q_ref, qd_ref, qu_ref), merge(k_ref, kd_ref, ku_ref), merge(v_ref, vd_ref, vu_ref)
    for n in range(joined_ref.shape[1] // QKV):
        base = n * QKV
        joined_ref[:, base : base + OUT] = q[:, n * OUT : (n + 1) * OUT]
        joined_ref[:, base + OUT : base + OUT + DH] = k[:, n * DH : (n + 1) * DH]
        joined_ref[:, base + OUT + DH : base + QKV] = v[:, n * DH : (n + 1) * DH]
    merged_ref[...] = merge(o_ref, od_ref, ou_ref)
    widened = states_ref[...].astype(jnp.float32)
    squared_average = jnp.mean(widened * widened, axis=-1, keepdims=True)
    normed = widened * lax.rsqrt(squared_average + epsilon) * gain_ref[...].reshape(1, 1, -1)
    normed_ref[...] = normed.reshape(normed_ref.shape).astype(jnp.bfloat16)


def prepare(slot, gain, states, bases, downs, ups):
    steps = 2
    seqs, decode, width = states.shape
    block = seqs // steps

    def cols(array):
        return pl.BlockSpec((array.shape[0], array.shape[1] // steps), lambda i, s: (0, i))

    def down(array):
        return pl.BlockSpec((1, *array.shape[1:]), lambda i, s: (s[0], 0, 0))

    def up(array):
        return pl.BlockSpec((1, array.shape[1], array.shape[2] // steps), lambda i, s: (s[0], 0, i))

    return pl.pallas_call(
        prepare_kernel,
        out_shape=(
            jax.ShapeDtypeStruct((seqs * decode, width), jnp.bfloat16),
            jax.ShapeDtypeStruct((WROWS, QKV * 8), jnp.bfloat16),
            jax.ShapeDtypeStruct((WROWS, OUT * 8), jnp.bfloat16),
        ),
        grid_spec=pltpu.PrefetchScalarGridSpec(
            num_scalar_prefetch=1,
            grid=(steps,),
            in_specs=[
                pl.BlockSpec((1, width), lambda i, s: (0, 0)),
                pl.BlockSpec((block, decode, width), lambda i, s: (i, 0, 0)),
                *[cols(b) for b in bases],
                *[down(d) for d in downs],
                *[up(u) for u in ups],
            ],
            out_specs=(
                pl.BlockSpec((block * decode, width), lambda i, s: (i, 0)),
                pl.BlockSpec((WROWS, QKV * 8 // steps), lambda i, s: (0, i)),
                pl.BlockSpec((WROWS, OUT * 8 // steps), lambda i, s: (0, i)),
            ),
        ),
        name="prepare",
    )(slot, gain.reshape(1, -1), states, *bases, *downs, *ups)


def rope_tables(positions):
    half_dim = DH // 2
    frequency = rope_theta ** (-2.0 * jnp.arange(half_dim, dtype=jnp.float32) / DH)
    rotation_phases = positions[:, None] * frequency[None, :]
    cosine, sine = jnp.cos(rotation_phases), jnp.sin(rotation_phases)
    return jnp.concatenate((cosine, cosine), -1), jnp.concatenate((-sine, sine), -1)


def local(
    states,
    norm_gain,
    query_base,
    key_base,
    value_base,
    output_base,
    query_down,
    query_up,
    key_down,
    key_up,
    value_down,
    value_up,
    output_down,
    output_up,
    adapter_layer,
    kv_lengths,
    cache_keys,
    cache_values,
):
    seq_count, step_count, _ = states.shape
    normed, joined, merged_output = prepare(
        adapter_layer,
        norm_gain,
        states,
        (query_base, key_base, value_base, output_base),
        (query_down, key_down, value_down, output_down),
        (query_up, key_up, value_up, output_up),
    )
    positions = (
        kv_lengths.astype(jnp.float32)[:, None] + jnp.arange(step_count, dtype=jnp.float32)[None, :]
    )
    cosine, sine = rope_tables(positions.reshape(-1))
    keys = cache_keys.reshape(seq_count, -1, DH)
    values = cache_values.reshape(seq_count, -1, DH)
    return run_layer(normed, joined, merged_output, cosine, sine, kv_lengths, keys, values)


def solution(mesh):
    in_specs = (
        P("fsdp", None, None),
        P(),
        P(("fsdp", "tp"), None),
        P(("fsdp", "tp"), None),
        P(("fsdp", "tp"), None),
        P(("fsdp", "tp"), None),
        P(None, ("fsdp", "tp"), None),
        P(),
        P(None, ("fsdp", "tp"), None),
        P(),
        P(None, ("fsdp", "tp"), None),
        P(),
        P(None, ("fsdp", "tp"), None),
        P(),
        P(),
        P("fsdp"),
        P("fsdp", None, "tp", None),
        P("fsdp", None, "tp", None),
    )
    out_specs = P("fsdp", None, "tp")
    return jax.shard_map(local, mesh=mesh, in_specs=in_specs, out_specs=out_specs, check_vma=False)
```

```python
import functools

import jax
import jax.numpy as jnp
from jax import lax
from jax.experimental import pallas as pl
from jax.experimental.pallas import tpu as pltpu
from jax.sharding import PartitionSpec as P

HQ = 64
KVH = 8
DH = 128
LEN = 512
STEPS = 4
MESH = pl.DeviceIdType.MESH

rope_theta = 1000000.0
low_rank_scale = 0.5
epsilon = 1e-06

TOK = 128
WROWS = 64
PLANE = 2048
QKV = 1280
OUT = 1024
CW = 256
NC = QKV // CW
NO = OUT // CW


def coords():
    f = lax.axis_index("fsdp")
    t = lax.axis_index("tp")
    return f // 4, lax.rem(f // 2, 2), lax.rem(f, 2), t


def flip(v, bit):
    return 1 - v if bit else v


def xor_z(z, e):
    hi, lo = z // 2, lax.rem(z, 2)
    return flip(hi, e >> 1) * 2 + flip(lo, e & 1)


def xor_t(t, d):
    b2, b1, b0 = t // 4, lax.rem(t // 2, 2), lax.rem(t, 2)
    return flip(b2, (d >> 2) & 1) * 4 + flip(b1, (d >> 1) & 1) * 2 + flip(b0, d & 1)


def dev(z, xl, c, t):
    return ((z * 2 + xl) * 2 + c, t)


def remote(src, dst, ssem, rsem, device):
    return pltpu.make_async_remote_copy(
        src_ref=src, dst_ref=dst, send_sem=ssem, recv_sem=rsem, device_id=device, device_id_type=MESH
    )


def layer_kernel(
    a_ref, w_ref, o_ref, cos_ref, sin_ref, len_ref, k_ref, v_ref, out_ref,
    abuf, wbuf, acc, cx, crecv, ostage, wo_ref, kbuf, vbuf, qbuf, knew, vnew, mixed, heads, hbuf, dsend, drecv,
    a_ss, a_rs, w1_ss, w1_rs, w2_ss, w2_rs, w3_ss, w3_rs, cx_ss, cx_rs, c_ss, c_rs,
    o1_ss, o1_rs, r1_ss, r1_rs, r2_ss, r2_rs, r3_ss, r3_rs,
    kv_s, h_ss, h_rs, d_ss, d_rs,
):
    z, xl, c, t = coords()
    xh = t // 4
    y = lax.rem(t, 4)
    xpart = dev(z, 1 - xl, c, t)
    ring = (dev(z, xl, c, xor_t(t, 1)), dev(z, xl, c, xor_t(t, 3)))

    def x_peer(d):
        return flip(xl, d & 1), flip(xh, d >> 1)
    cpart = dev(z, xl, 1 - c, t)

    def plane_peer(d):
        return dev(z, flip(xl, d >> 2), c, xor_t(t, d))

    def z_peer(e):
        return dev(xor_z(z, e), xl, c, t)

    zd = t // 2
    half = lax.rem(t, 2)

    y_to = lax.rem(z + 2 * (y // 2) + xh, 4)
    here = (z == zd) & (y == y_to)

    def h_target(d):
        lo, hi = x_peer(d)
        return dev(zd, lo, c, hi * 4 + y_to)

    z_rows = lax.rem(y + 8 - 2 * lax.rem(z, 2) - z // 2, 4)

    def h_source(i, h):
        return dev(z_rows, i, c, 2 * z + h)

    def d_target(i, j):
        return dev(z_rows, i, c, xh * 4 + 2 * xl + j)

    def d_source(p):
        return dev(p, y // 2, c, xh * 4 + lax.rem(z + 2 * (p % 2) + p // 2, 4))

    cache = [
        pltpu.make_async_copy(k_ref, kbuf, kv_s.at[0]),
        pltpu.make_async_copy(v_ref, vbuf, kv_s.at[1]),
    ]

    barrier = pltpu.get_barrier_semaphore()
    peers = [plane_peer(d) for d in range(1, 8)] + [z_peer(e) for e in range(1, 4)] + [xpart, cpart, dev(z, xl, c, xor_t(t, 4))]
    peers += [h_target(d) for d in range(4)] + [d_source(p) for p in range(4)]
    peers += [h_source(i, h) for i in range(2) for h in range(2)]
    peers += [d_target(i, j) for i in range(2) for j in range(2)]
    for p in peers:
        pl.semaphore_signal(barrier, inc=1, device_id=p, device_id_type=MESH)
    pl.semaphore_wait(barrier, len(peers))

    def a_copy(e):
        cols = pl.ds(pl.multiple_of(xor_z(z, e) * PLANE, PLANE), PLANE)
        if e == 0:
            return pltpu.make_async_copy(a_ref.at[:, cols], abuf.at[0], a_rs.at[0])
        return remote(a_ref.at[:, cols], abuf.at[e], a_ss.at[e], a_rs.at[e], z_peer(e))

    my_slot = (xl * 2 + c) * 8 + t

    def w1_copy(ch, d):
        td = xor_t(t, d)
        cols = pl.ds(pl.multiple_of(td * QKV + ch * CW, CW), CW)
        src = w_ref.at[:, cols]
        dst = wbuf.at[ch, my_slot]
        if d == 0:
            return pltpu.make_async_copy(src, dst, w1_rs.at[ch, 0])
        return remote(src, dst, w1_ss.at[ch, d], w1_rs.at[ch, d], plane_peer(d))

    def o_rows(source, d, core):
        lo, hi = x_peer(d)
        return wo_ref.at[(lo * 2 + core) * 8 + hi * 4 + xor_t(y, (0, 1, 3, 2)[source])]

    def o_mine(d):
        lo, hi = x_peer(d)
        return o_ref.at[:, pl.ds(pl.multiple_of((hi * 2 + lo) * 2 * OUT, 2 * OUT), 2 * OUT)]

    def o1_copy(d):
        if d == 0:
            return pltpu.make_async_copy(o_mine(0), ostage, o1_rs.at[0])
        lo, hi = x_peer(d)
        return remote(o_mine(d), wo_ref.at[my_slot], o1_ss.at[d], o1_rs.at[d], dev(z, lo, c, hi * 4 + y))

    def o1_wait(d):
        ref = o_rows(0, d, c)
        remote(ref, ref, o1_ss.at[d], o1_rs.at[d], xpart).wait_recv()

    def o_keep():
        return pltpu.make_async_copy(ostage, wo_ref.at[my_slot], o1_ss.at[0])

    def r1_copy(n, d):
        src = ostage if d == 0 else o_rows(0, d, c)
        return remote(src, o_rows(0, d, c), r1_ss.at[n, d], r1_rs.at[n, d], ring[n])

    def r1_wait(n, d):
        ref = o_rows(1 + n, d, c)
        remote(ref, ref, r1_ss.at[n, d], r1_rs.at[n, d], ring[n]).wait_recv()

    def r2_copy(d):
        n = d >> 1
        ref = o_rows(2 - n, d, c)
        return remote(ref, ref, r2_ss.at[d], r2_rs.at[d], ring[n])

    def r2_wait(d):
        ref = o_rows(3, d, c)
        remote(ref, ref, r2_ss.at[d], r2_rs.at[d], xpart).wait_recv()

    def r3_copy(source, d):
        ref = o_rows(source, d, c)
        src = ostage if (source, d) == (0, 0) else ref
        return remote(src, ref, r3_ss.at[source, d], r3_rs.at[source, d], cpart)

    def r3_wait(source, d):
        ref = o_rows(source, d, 1 - c)
        remote(ref, ref, r3_ss.at[source, d], r3_rs.at[source, d], cpart).wait_recv()

    def group_base(g, core):
        lo = xl if g in (0, 3) else 1 - xl
        hi = xh if g in (0, 2) else 1 - xh
        return (lo * 2 + core) * 8 + hi * 4

    def w2_copy(k, g):
        ref = wbuf.at[k, pl.ds(group_base(g, c), 4)]
        return remote(ref, ref, w2_ss.at[k, g], w2_rs.at[k, g], xpart)

    def w2_wait(k, g):
        ref = wbuf.at[k, pl.ds(group_base(g + 2, c), 4)]
        remote(ref, ref, w2_ss.at[k, g], w2_rs.at[k, g], xpart).wait_recv()

    def w3_copy(k, g):
        ref = wbuf.at[k, pl.ds(group_base(g, c), 4)]
        return remote(ref, ref, w3_ss.at[k, g], w3_rs.at[k, g], cpart)

    def w3_wait(k, g):
        ref = wbuf.at[k, pl.ds(group_base(g, 1 - c), 4)]
        remote(ref, ref, w3_ss.at[k, g], w3_rs.at[k, g], cpart).wait_recv()

    near = (1, 3)

    def cx_copy(ch, k):
        return remote(acc.at[ch, 2, k], cx.at[ch, k], cx_ss.at[ch, k], cx_rs.at[ch, k], z_peer(near[k]))

    def c_copy(ch, n, k):
        return remote(
            acc.at[ch, near[n], k], crecv.at[ch, n, k], c_ss.at[ch, n, k], c_rs.at[ch, n, k], z_peer(near[n])
        )

    def combine(ch):
        for k in range(2):
            cx_copy(ch, k).wait_recv()
            n = 1 - k
            acc[ch, near[n], k] = acc[ch, near[n], k] + cx[ch, k]
            c_copy(ch, n, k).start()

    def start_w1(ch, carry):
        for d in range(8):
            w1_copy(ch, d).start()
        return carry

    start_w1(0, 0)
    for e in (1, 3, 2, 0):
        a_copy(e).start()
    o1_copy(0).start()
    for copy in cache:
        copy.start()
    lax.fori_loop(1, NC, start_w1, 0)
    for d in (1, 3, 2):
        o1_copy(d).start()

    def relay(k):
        for g in range(2):
            for d in range(g * 4, g * 4 + 4):
                source_slot = (flip(xl, d >> 2) * 2 + c) * 8 + xor_t(t, d)
                if d == 0:
                    w1_copy(k, 0).wait()
                else:
                    ref = wbuf.at[k, source_slot]
                    remote(ref, ref, w1_ss.at[k, d], w1_rs.at[k, d], plane_peer(d)).wait_recv()
            w2_copy(k, g).start()
            w3_copy(k, g).start()

    def share(k):
        for g in range(2):
            w2_wait(k, g)
            w3_copy(k, g + 2).start()

    def multiply(ch):
        for g in range(4):
            w3_wait(ch, g)
        rows = abuf[...].reshape(4 * TOK, PLANE)
        part = jnp.dot(rows, wbuf[ch].reshape(PLANE, CW), preferred_element_type=jnp.float32)
        part = part.reshape(4, TOK, CW)
        acc[ch, :, 0] = part[:, :, :DH]
        acc[ch, :, 1] = part[:, :, DH:]
        for k in range(2):
            cx_copy(ch, k).start()
            c_copy(ch, k, k).start()

    def spread(d):
        o1_wait(d)
        r1_copy(0, d).start()
        r1_copy(1, d).start()
        r3_copy(0, d).start()

    def forward(d):
        n = d >> 1
        r1_wait(1 - n, d)
        r2_copy(d).start()
        r3_copy(2 - n, d).start()

    def keep(d):
        n = 1 - (d >> 1)
        r1_wait(1 - n, d)
        r3_copy(2 - n, d).start()

    relay(0)
    o1_copy(0).wait()
    r1_copy(0, 0).start()
    r1_copy(1, 0).start()
    r3_copy(0, 0).start()
    o_keep().start()
    relay(1)
    share(0)
    spread(1)
    relay(2)
    share(1)
    spread(3)
    relay(3)
    share(2)
    spread(2)
    relay(4)
    a_copy(0).wait()
    for e in (1, 3, 2):
        a_copy(e).wait_recv()
    multiply(0)
    multiply(1)
    forward(0)
    keep(0)
    multiply(2)
    combine(0)
    share(3)
    forward(1)
    keep(1)
    multiply(3)
    combine(1)
    share(4)
    multiply(4)
    forward(3)
    keep(3)
    combine(2)
    forward(2)
    keep(2)
    combine(3)
    combine(4)

    def rope(values):
        return values * cos_ref[...] + pltpu.roll(values, DH // 2, axis=1) * sin_ref[...]

    for ch in range(NC):
        for n in range(2):
            for k in range(2):
                c_copy(ch, n, k).wait_recv()
        first, second = [acc[ch, 0, k] + crecv[ch, 0, k] + crecv[ch, 1, k] for k in range(2)]
        if ch < NC - 1:
            qbuf[2 * ch] = rope(first).astype(jnp.bfloat16).astype(jnp.float32)
            qbuf[2 * ch + 1] = rope(second).astype(jnp.bfloat16).astype(jnp.float32)
        else:
            knew[...] = rope(first).astype(jnp.bfloat16)
            vnew[...] = second.astype(jnp.bfloat16)
    for copy in cache:
        copy.wait()

    score_scale = DH ** (-0.5)
    contract_last = (((1,), (1,)), ((), ()))

    def attend_pair(p):
        tokens = pl.ds(pl.multiple_of(p * 8, 8), 8)
        queries = qbuf[:, tokens, :].reshape(64, DH).astype(jnp.bfloat16)
        keys = kbuf[pl.ds(2 * p, 2)].reshape(2 * LEN, DH)
        values = vbuf[pl.ds(2 * p, 2)].reshape(2 * LEN, DH)
        token = lax.rem(lax.broadcasted_iota(jnp.int32, (64, 1), 0), 8)
        second = token >= STEPS
        low = jnp.where(second, LEN, 0)
        high = low + jnp.where(second, len_ref[2 * p + 1], len_ref[2 * p])
        slot = lax.broadcasted_iota(jnp.int32, (64, 2 * LEN), 1)
        old = lax.dot_general(queries, keys, contract_last, preferred_element_type=jnp.float32) * score_scale
        old = jnp.where((slot >= low) & (slot < high), old, -1e30)
        column = lax.broadcasted_iota(jnp.int32, (64, TOK), 1)
        last = p * 8 + token
        begin = p * 8 + jnp.where(second, STEPS, 0)
        new = lax.dot_general(queries, knew[...], contract_last, preferred_element_type=jnp.float32) * score_scale
        new = jnp.where((column >= begin) & (column <= last), new, -1e30)
        highest = jnp.maximum(jnp.max(old, -1, keepdims=True), jnp.max(new, -1, keepdims=True))
        old_exp = jnp.exp(old - highest)
        new_exp = jnp.exp(new - highest)
        inverse = 1.0 / (jnp.sum(old_exp, -1, keepdims=True) + jnp.sum(new_exp, -1, keepdims=True))
        old_weights = (old_exp * inverse).astype(jnp.bfloat16)
        new_weights = (new_exp * inverse).astype(jnp.bfloat16)
        mixture = jnp.dot(old_weights, values, preferred_element_type=jnp.float32)
        mixture = mixture + jnp.dot(new_weights, vnew[...], preferred_element_type=jnp.float32)
        for g in range(8):
            mixed[tokens, g * DH : (g + 1) * DH] = mixture[g * 8 : (g + 1) * 8]

    QT = TOK // 4

    def h_rows(qt):
        return heads.at[pl.ds(pl.multiple_of(qt * QT, QT), QT)]

    def h_slot(qt):
        return hbuf.at[xl, pl.ds(pl.multiple_of(qt * QT, QT), QT), pl.ds(pl.multiple_of(half * OUT, OUT), OUT)]

    def h_send(qt, d):
        return remote(h_rows(qt), h_slot(qt), h_ss.at[qt, d], h_rs.at[xl, half, qt], h_target(d))

    def h_local(qt):
        return pltpu.make_async_copy(h_rows(qt), h_slot(qt), h_rs.at[xl, half, qt])

    def quarter(qt, carry):
        for n in range(4):
            attend_pair(qt * 4 + n)
        rows = pl.ds(pl.multiple_of(qt * QT, QT), QT)
        heads[rows] = mixed[rows].astype(jnp.bfloat16)
        for d in (2, 1, 3):
            h_send(qt, d).start()

        @pl.when(here)
        def _():
            h_local(qt).start()

        @pl.when(jnp.logical_not(here))
        def _():
            h_send(qt, 0).start()

        return carry

    lax.fori_loop(0, 4, quarter, 0)

    for d in (0, 1, 3, 2):
        r2_wait(d)
        r3_copy(3, d).start()
    for source in range(4):
        for d in range(4):
            r3_wait(source, d)
    o_keep().wait()

    for i in range(2):
        for h in range(2):
            for qt in range(4):
                ref = hbuf.at[i, pl.ds(qt * QT, QT), pl.ds(h * OUT, OUT)]
                pltpu.make_async_copy(ref, ref, h_rs.at[i, h, qt]).wait()

    def mine(i, j):
        return (z_rows == z) & (xl == i) & (y == 2 * xl + j)

    def d_copy(n, j, i):
        return remote(
            dsend.at[j, n, i], drecv.at[n, z], d_ss.at[j, n, i], d_rs.at[n, z], d_target(i, j)
        )

    def d_local(n, j, i):
        return pltpu.make_async_copy(dsend.at[j, n, i], drecv.at[n, z], d_rs.at[n, z])

    for n in range(NO):
        for j in range(2):
            lo = j * OUT + n * CW
            w = wo_ref[:, :, lo : lo + CW].reshape(PLANE, CW)
            part = jnp.dot(hbuf[...].reshape(2 * TOK, PLANE), w, preferred_element_type=jnp.float32)
            dsend[j, n] = part.astype(jnp.bfloat16).reshape(2, TOK, CW)
            for i in range(2):

                @pl.when(mine(i, j))
                def _():
                    d_local(n, j, i).start()

                @pl.when(jnp.logical_not(mine(i, j)))
                def _():
                    d_copy(n, j, i).start()

    for n in range(NO):
        total = None
        for p in range(4):
            ref = drecv.at[n, p]
            pltpu.make_async_copy(ref, ref, d_rs.at[n, p]).wait()
            part = drecv[n, p].astype(jnp.float32)
            total = part if total is None else total + part
        out_ref[:, :, n * CW : (n + 1) * CW] = total.reshape(TOK // STEPS, STEPS, CW).astype(jnp.bfloat16)

    def drain_heads(qt, carry):
        for d in range(1, 4):
            h_send(qt, d).wait_send()

        @pl.when(jnp.logical_not(here))
        def _():
            h_send(qt, 0).wait_send()

        return carry

    lax.fori_loop(0, 4, drain_heads, 0)
    for n in range(NO):
        for j in range(2):
            for i in range(2):

                @pl.when(jnp.logical_not(mine(i, j)))
                def _():
                    d_copy(n, j, i).wait_send()

    for e in range(1, 4):
        a_copy(e).wait_send()

    def drain(ch, carry):
        for d in range(1, 8):
            w1_copy(ch, d).wait_send()
        for g in range(2):
            w2_copy(ch, g).wait_send()
        for g in range(4):
            w3_copy(ch, g).wait_send()
        for k in range(2):
            cx_copy(ch, k).wait_send()
            for n in range(2):
                c_copy(ch, n, k).wait_send()
        return carry

    lax.fori_loop(0, NC, drain, 0)
    for d in range(1, 4):
        o1_copy(d).wait_send()
    for d in range(4):
        r1_copy(0, d).wait_send()
        r1_copy(1, d).wait_send()
        r2_copy(d).wait_send()
        for source in range(4):
            r3_copy(source, d).wait_send()


VM = pl.BlockSpec(memory_space=pltpu.VMEM)
ANY = pl.BlockSpec(memory_space=pl.ANY)
DMA = pltpu.SemaphoreType.DMA


def run_layer(normed, joined, merged_output, cosine, sine, lengths, keys, values):
    return pl.pallas_call(
        layer_kernel,
        out_shape=jax.ShapeDtypeStruct((TOK // STEPS, STEPS, OUT), jnp.bfloat16),
        in_specs=[ANY, ANY, ANY, VM, VM, pl.BlockSpec(memory_space=pltpu.SMEM), ANY, ANY],
        out_specs=VM,
        scratch_shapes=[
            pltpu.VMEM((4, TOK, PLANE), jnp.bfloat16),
            pltpu.VMEM((NC, 32, WROWS, CW), jnp.bfloat16),
            pltpu.VMEM((NC, 4, 2, TOK, DH), jnp.float32),
            pltpu.VMEM((NC, 2, TOK, DH), jnp.float32),
            pltpu.VMEM((NC, 2, 2, TOK, DH), jnp.float32),
            pltpu.VMEM((WROWS, 2 * OUT), jnp.bfloat16),
            pltpu.VMEM((32, WROWS, 2 * OUT), jnp.bfloat16),
            pltpu.VMEM(keys.shape, jnp.bfloat16),
            pltpu.VMEM(values.shape, jnp.bfloat16),
            pltpu.VMEM((8, TOK, DH), jnp.float32),
            pltpu.VMEM((TOK, DH), jnp.bfloat16),
            pltpu.VMEM((TOK, DH), jnp.bfloat16),
            pltpu.VMEM((TOK, OUT), jnp.float32),
            pltpu.VMEM((TOK, OUT), jnp.bfloat16),
            pltpu.VMEM((2, TOK, PLANE), jnp.bfloat16),
            pltpu.VMEM((2, NO, 2, TOK, CW), jnp.bfloat16),
            pltpu.VMEM((NO, 4, TOK, CW), jnp.bfloat16),
            DMA((4,)), DMA((4,)),
            DMA((NC, 8)), DMA((NC, 8)),
            DMA((NC, 2)), DMA((NC, 2)),
            DMA((NC, 4)), DMA((NC, 4)),
            DMA((NC, 2)), DMA((NC, 2)),
            DMA((NC, 2, 2)), DMA((NC, 2, 2)),
            DMA((4,)), DMA((4,)),
            DMA((2, 4)), DMA((2, 4)),
            DMA((4,)), DMA((4,)),
            DMA((4, 4)), DMA((4, 4)),
            DMA((2,)),
            DMA((4, 4)), DMA((2, 2, 4)),
            DMA((2, NO, 2)), DMA((NO, 4)),
        ],
        compiler_params=pltpu.CompilerParams(collective_id=0, has_side_effects=True, vmem_limit_bytes=62 << 20),
        name="layer",
    )(normed, joined, merged_output, cosine, sine, lengths, keys, values)


def prepare_kernel(
    slot_ref, gain_ref, states_ref, q_ref, k_ref, v_ref, o_ref,
    qd_ref, kd_ref, vd_ref, od_ref, qu_ref, ku_ref, vu_ref, ou_ref,
    normed_ref, joined_ref, merged_ref,
):
    def merge(base, down, up):
        delta = jnp.dot(down[0], up[0], preferred_element_type=jnp.float32)
        return (base[...].astype(jnp.float32) + low_rank_scale * delta).astype(jnp.bfloat16)

    q, k, v = merge(q_ref, qd_ref, qu_ref), merge(k_ref, kd_ref, ku_ref), merge(v_ref, vd_ref, vu_ref)
    for n in range(joined_ref.shape[1] // QKV):
        base = n * QKV
        joined_ref[:, base : base + OUT] = q[:, n * OUT : (n + 1) * OUT]
        joined_ref[:, base + OUT : base + OUT + DH] = k[:, n * DH : (n + 1) * DH]
        joined_ref[:, base + OUT + DH : base + QKV] = v[:, n * DH : (n + 1) * DH]
    merged_ref[...] = merge(o_ref, od_ref, ou_ref)
    widened = states_ref[...].astype(jnp.float32)
    squared_average = jnp.mean(widened * widened, axis=-1, keepdims=True)
    normed = widened * lax.rsqrt(squared_average + epsilon) * gain_ref[...].reshape(1, 1, -1)
    normed_ref[...] = normed.reshape(normed_ref.shape).astype(jnp.bfloat16)


def prepare(slot, gain, states, bases, downs, ups):
    steps = 2
    seqs, decode, width = states.shape
    block = seqs // steps

    def cols(array):
        return pl.BlockSpec((array.shape[0], array.shape[1] // steps), lambda i, s: (0, i))

    def down(array):
        return pl.BlockSpec((1, *array.shape[1:]), lambda i, s: (s[0], 0, 0))

    def up(array):
        return pl.BlockSpec((1, array.shape[1], array.shape[2] // steps), lambda i, s: (s[0], 0, i))

    return pl.pallas_call(
        prepare_kernel,
        out_shape=(
            jax.ShapeDtypeStruct((seqs * decode, width), jnp.bfloat16),
            jax.ShapeDtypeStruct((WROWS, QKV * 8), jnp.bfloat16),
            jax.ShapeDtypeStruct((WROWS, OUT * 8), jnp.bfloat16),
        ),
        grid_spec=pltpu.PrefetchScalarGridSpec(
            num_scalar_prefetch=1,
            grid=(steps,),
            in_specs=[
                pl.BlockSpec((1, width), lambda i, s: (0, 0)),
                pl.BlockSpec((block, decode, width), lambda i, s: (i, 0, 0)),
                *[cols(b) for b in bases],
                *[down(d) for d in downs],
                *[up(u) for u in ups],
            ],
            out_specs=(
                pl.BlockSpec((block * decode, width), lambda i, s: (i, 0)),
                pl.BlockSpec((WROWS, QKV * 8 // steps), lambda i, s: (0, i)),
                pl.BlockSpec((WROWS, OUT * 8 // steps), lambda i, s: (0, i)),
            ),
        ),
        name="prepare",
    )(slot, gain.reshape(1, -1), states, *bases, *downs, *ups)


def rope_tables(positions):
    half_dim = DH // 2
    frequency = rope_theta ** (-2.0 * jnp.arange(half_dim, dtype=jnp.float32) / DH)
    rotation_phases = positions[:, None] * frequency[None, :]
    cosine, sine = jnp.cos(rotation_phases), jnp.sin(rotation_phases)
    return jnp.concatenate((cosine, cosine), -1), jnp.concatenate((-sine, sine), -1)


def local(
    states,
    norm_gain,
    query_base,
    key_base,
    value_base,
    output_base,
    query_down,
    query_up,
    key_down,
    key_up,
    value_down,
    value_up,
    output_down,
    output_up,
    adapter_layer,
    kv_lengths,
    cache_keys,
    cache_values,
):
    seq_count, step_count, _ = states.shape
    normed, joined, merged_output = prepare(
        adapter_layer,
        norm_gain,
        states,
        (query_base, key_base, value_base, output_base),
        (query_down, key_down, value_down, output_down),
        (query_up, key_up, value_up, output_up),
    )
    positions = (
        kv_lengths.astype(jnp.float32)[:, None] + jnp.arange(step_count, dtype=jnp.float32)[None, :]
    )
    cosine, sine = rope_tables(positions.reshape(-1))
    keys = cache_keys.reshape(seq_count, -1, DH)
    values = cache_values.reshape(seq_count, -1, DH)
    return run_layer(normed, joined, merged_output, cosine, sine, kv_lengths, keys, values)


def solution(mesh):
    in_specs = (
        P("fsdp", None, None),
        P(),
        P(("fsdp", "tp"), None),
        P(("fsdp", "tp"), None),
        P(("fsdp", "tp"), None),
        P(("fsdp", "tp"), None),
        P(None, ("fsdp", "tp"), None),
        P(),
        P(None, ("fsdp", "tp"), None),
        P(),
        P(None, ("fsdp", "tp"), None),
        P(),
        P(None, ("fsdp", "tp"), None),
        P(),
        P(),
        P("fsdp"),
        P("fsdp", None, "tp", None),
        P("fsdp", None, "tp", None),
    )
    out_specs = P("fsdp", None, "tp")
    return jax.shard_map(local, mesh=mesh, in_specs=in_specs, out_specs=out_specs, check_vma=False)
```

```python
import functools

import jax
import jax.numpy as jnp
from jax import lax
from jax.experimental import pallas as pl
from jax.experimental.pallas import tpu as pltpu
from jax.sharding import PartitionSpec as P

HQ = 64
KVH = 8
DH = 128
LEN = 512
STEPS = 4
MESH = pl.DeviceIdType.MESH

rope_theta = 1000000.0
low_rank_scale = 0.5
epsilon = 1e-06

TOK = 128
WROWS = 64
PLANE = 2048
QKV = 1280
OUT = 1024
CW = 256
NC = QKV // CW
NO = OUT // CW


def coords():
    f = lax.axis_index("fsdp")
    t = lax.axis_index("tp")
    return f // 4, lax.rem(f // 2, 2), lax.rem(f, 2), t


def flip(v, bit):
    return 1 - v if bit else v


def xor_z(z, e):
    hi, lo = z // 2, lax.rem(z, 2)
    return flip(hi, e >> 1) * 2 + flip(lo, e & 1)


def xor_t(t, d):
    b2, b1, b0 = t // 4, lax.rem(t // 2, 2), lax.rem(t, 2)
    return flip(b2, (d >> 2) & 1) * 4 + flip(b1, (d >> 1) & 1) * 2 + flip(b0, d & 1)


def dev(z, xl, c, t):
    return ((z * 2 + xl) * 2 + c, t)


def remote(src, dst, ssem, rsem, device):
    return pltpu.make_async_remote_copy(
        src_ref=src, dst_ref=dst, send_sem=ssem, recv_sem=rsem, device_id=device, device_id_type=MESH
    )


def layer_kernel(
    a_ref, w_ref, o_ref, cos_ref, sin_ref, len_ref, k_ref, v_ref, out_ref,
    abuf, wbuf, acc, cx, crecv, ostage, wo_ref, kbuf, vbuf, qbuf, knew, vnew, mixed, heads, hbuf, dsend, drecv,
    a_ss, a_rs, w1_ss, w1_rs, w2_ss, w2_rs, w3_ss, w3_rs, cx_ss, cx_rs, c_ss, c_rs,
    o1_ss, o1_rs, r1_ss, r1_rs, r2_ss, r2_rs, r3_ss, r3_rs,
    kv_s, h_ss, h_rs, d_ss, d_rs,
):
    z, xl, c, t = coords()
    xh = t // 4
    y = lax.rem(t, 4)
    xpart = dev(z, 1 - xl, c, t)
    ring = (dev(z, xl, c, xor_t(t, 1)), dev(z, xl, c, xor_t(t, 3)))

    def x_peer(d):
        return flip(xl, d & 1), flip(xh, d >> 1)
    cpart = dev(z, xl, 1 - c, t)

    def plane_peer(d):
        return dev(z, flip(xl, d >> 2), c, xor_t(t, d))

    def z_peer(e):
        return dev(xor_z(z, e), xl, c, t)

    zd = t // 2
    half = lax.rem(t, 2)

    y_to = lax.rem(z + 2 * (y // 2) + xh, 4)
    here = (z == zd) & (y == y_to)

    def h_target(d):
        lo, hi = x_peer(d)
        return dev(zd, lo, c, hi * 4 + y_to)

    z_rows = lax.rem(y + 8 - 2 * lax.rem(z, 2) - z // 2, 4)

    def h_source(i, h):
        return dev(z_rows, i, c, 2 * z + h)

    def d_target(i, j):
        return dev(z_rows, i, c, xh * 4 + 2 * xl + j)

    def d_source(p):
        return dev(p, y // 2, c, xh * 4 + lax.rem(z + 2 * (p % 2) + p // 2, 4))

    cache = [
        pltpu.make_async_copy(k_ref, kbuf, kv_s.at[0]),
        pltpu.make_async_copy(v_ref, vbuf, kv_s.at[1]),
    ]

    barrier = pltpu.get_barrier_semaphore()
    peers = [plane_peer(d) for d in range(1, 8)] + [z_peer(e) for e in range(1, 4)] + [xpart, cpart, dev(z, xl, c, xor_t(t, 4))]
    peers += [h_target(d) for d in range(4)] + [d_source(p) for p in range(4)]
    peers += [h_source(i, h) for i in range(2) for h in range(2)]
    peers += [d_target(i, j) for i in range(2) for j in range(2)]
    for p in peers:
        pl.semaphore_signal(barrier, inc=1, device_id=p, device_id_type=MESH)
    pl.semaphore_wait(barrier, len(peers))

    def a_copy(e):
        cols = pl.ds(pl.multiple_of(xor_z(z, e) * PLANE, PLANE), PLANE)
        if e == 0:
            return pltpu.make_async_copy(a_ref.at[:, cols], abuf.at[0], a_rs.at[0])
        return remote(a_ref.at[:, cols], abuf.at[e], a_ss.at[e], a_rs.at[e], z_peer(e))

    my_slot = (xl * 2 + c) * 8 + t

    def w1_copy(ch, d):
        td = xor_t(t, d)
        cols = pl.ds(pl.multiple_of(td * QKV + ch * CW, CW), CW)
        src = w_ref.at[:, cols]
        dst = wbuf.at[ch, my_slot]
        if d == 0:
            return pltpu.make_async_copy(src, dst, w1_rs.at[ch, 0])
        return remote(src, dst, w1_ss.at[ch, d], w1_rs.at[ch, d], plane_peer(d))

    def o_rows(source, d, core):
        lo, hi = x_peer(d)
        return wo_ref.at[(lo * 2 + core) * 8 + hi * 4 + xor_t(y, (0, 1, 3, 2)[source])]

    def o_mine(d):
        lo, hi = x_peer(d)
        return o_ref.at[:, pl.ds(pl.multiple_of((hi * 2 + lo) * 2 * OUT, 2 * OUT), 2 * OUT)]

    def o1_copy(d):
        if d == 0:
            return pltpu.make_async_copy(o_mine(0), ostage, o1_rs.at[0])
        lo, hi = x_peer(d)
        return remote(o_mine(d), wo_ref.at[my_slot], o1_ss.at[d], o1_rs.at[d], dev(z, lo, c, hi * 4 + y))

    def o1_wait(d):
        ref = o_rows(0, d, c)
        remote(ref, ref, o1_ss.at[d], o1_rs.at[d], xpart).wait_recv()

    def o_keep():
        return pltpu.make_async_copy(ostage, wo_ref.at[my_slot], o1_ss.at[0])

    def r1_copy(n, d):
        src = ostage if d == 0 else o_rows(0, d, c)
        return remote(src, o_rows(0, d, c), r1_ss.at[n, d], r1_rs.at[n, d], ring[n])

    def r1_wait(n, d):
        ref = o_rows(1 + n, d, c)
        remote(ref, ref, r1_ss.at[n, d], r1_rs.at[n, d], ring[n]).wait_recv()

    def r2_copy(d):
        n = d >> 1
        ref = o_rows(2 - n, d, c)
        return remote(ref, ref, r2_ss.at[d], r2_rs.at[d], ring[n])

    def r2_wait(d):
        ref = o_rows(3, d, c)
        remote(ref, ref, r2_ss.at[d], r2_rs.at[d], xpart).wait_recv()

    def r3_copy(source, d):
        ref = o_rows(source, d, c)
        src = ostage if (source, d) == (0, 0) else ref
        return remote(src, ref, r3_ss.at[source, d], r3_rs.at[source, d], cpart)

    def r3_wait(source, d):
        ref = o_rows(source, d, 1 - c)
        remote(ref, ref, r3_ss.at[source, d], r3_rs.at[source, d], cpart).wait_recv()

    def group_base(g, core):
        lo = xl if g in (0, 3) else 1 - xl
        hi = xh if g in (0, 2) else 1 - xh
        return (lo * 2 + core) * 8 + hi * 4

    def w2_copy(k, g):
        ref = wbuf.at[k, pl.ds(group_base(g, c), 4)]
        return remote(ref, ref, w2_ss.at[k, g], w2_rs.at[k, g], xpart)

    def w2_wait(k, g):
        ref = wbuf.at[k, pl.ds(group_base(g + 2, c), 4)]
        remote(ref, ref, w2_ss.at[k, g], w2_rs.at[k, g], xpart).wait_recv()

    def w3_copy(k, g):
        ref = wbuf.at[k, pl.ds(group_base(g, c), 4)]
        return remote(ref, ref, w3_ss.at[k, g], w3_rs.at[k, g], cpart)

    def w3_wait(k, g):
        ref = wbuf.at[k, pl.ds(group_base(g, 1 - c), 4)]
        remote(ref, ref, w3_ss.at[k, g], w3_rs.at[k, g], cpart).wait_recv()

    near = (1, 3)

    def cx_copy(ch, k):
        return remote(acc.at[ch, 2, k], cx.at[ch, k], cx_ss.at[ch, k], cx_rs.at[ch, k], z_peer(near[k]))

    def c_copy(ch, n, k):
        return remote(
            acc.at[ch, near[n], k], crecv.at[ch, n, k], c_ss.at[ch, n, k], c_rs.at[ch, n, k], z_peer(near[n])
        )

    def combine(ch):
        for k in range(2):
            cx_copy(ch, k).wait_recv()
            n = 1 - k
            acc[ch, near[n], k] = acc[ch, near[n], k] + cx[ch, k]
            c_copy(ch, n, k).start()

    def start_w1(ch, carry):
        for d in range(8):
            w1_copy(ch, d).start()
        return carry

    start_w1(0, 0)
    for e in (1, 3, 2, 0):
        a_copy(e).start()
    o1_copy(0).start()
    for copy in cache:
        copy.start()
    lax.fori_loop(1, NC, start_w1, 0)
    for d in (1, 3, 2):
        o1_copy(d).start()

    def relay(k):
        for g in range(2):
            for d in range(g * 4, g * 4 + 4):
                source_slot = (flip(xl, d >> 2) * 2 + c) * 8 + xor_t(t, d)
                if d == 0:
                    w1_copy(k, 0).wait()
                else:
                    ref = wbuf.at[k, source_slot]
                    remote(ref, ref, w1_ss.at[k, d], w1_rs.at[k, d], plane_peer(d)).wait_recv()
            w2_copy(k, g).start()
            w3_copy(k, g).start()

    def share(k):
        for g in range(2):
            w2_wait(k, g)
            w3_copy(k, g + 2).start()

    def multiply(ch):
        for g in range(4):
            w3_wait(ch, g)
        rows = abuf[...].reshape(4 * TOK, PLANE)
        part = jnp.dot(rows, wbuf[ch].reshape(PLANE, CW), preferred_element_type=jnp.float32)
        part = part.reshape(4, TOK, CW)
        acc[ch, :, 0] = part[:, :, :DH]
        acc[ch, :, 1] = part[:, :, DH:]
        for k in range(2):
            cx_copy(ch, k).start()
            c_copy(ch, k, k).start()

    def spread(d):
        o1_wait(d)
        r1_copy(0, d).start()
        r1_copy(1, d).start()
        r3_copy(0, d).start()

    def forward(d):
        n = d >> 1
        r1_wait(1 - n, d)
        r2_copy(d).start()
        r3_copy(2 - n, d).start()

    def keep(d):
        n = 1 - (d >> 1)
        r1_wait(1 - n, d)
        r3_copy(2 - n, d).start()

    relay(0)
    o1_copy(0).wait()
    r1_copy(0, 0).start()
    r1_copy(1, 0).start()
    r3_copy(0, 0).start()
    o_keep().start()
    relay(1)
    share(0)
    spread(1)
    relay(2)
    share(1)
    spread(3)
    relay(3)
    share(2)
    spread(2)
    relay(4)
    a_copy(0).wait()
    for e in (1, 3, 2):
        a_copy(e).wait_recv()
    multiply(0)
    multiply(1)
    forward(0)
    keep(0)
    multiply(2)
    combine(0)
    share(3)
    forward(1)
    keep(1)
    multiply(3)
    combine(1)
    share(4)
    multiply(4)
    forward(3)
    keep(3)
    combine(2)
    forward(2)
    keep(2)
    combine(3)
    combine(4)

    def rope(values):
        return values * cos_ref[...] + pltpu.roll(values, DH // 2, axis=1) * sin_ref[...]

    for ch in range(NC):
        for n in range(2):
            for k in range(2):
                c_copy(ch, n, k).wait_recv()
        first, second = [acc[ch, 0, k] + crecv[ch, 0, k] + crecv[ch, 1, k] for k in range(2)]
        if ch < NC - 1:
            qbuf[2 * ch] = rope(first).astype(jnp.bfloat16).astype(jnp.float32)
            qbuf[2 * ch + 1] = rope(second).astype(jnp.bfloat16).astype(jnp.float32)
        else:
            knew[...] = rope(first).astype(jnp.bfloat16)
            vnew[...] = second.astype(jnp.bfloat16)
    for copy in cache:
        copy.wait()

    score_scale = DH ** (-0.5)
    contract_last = (((1,), (1,)), ((), ()))

    def attend_pair(p):
        tokens = pl.ds(pl.multiple_of(p * 8, 8), 8)
        queries = qbuf[:, tokens, :].reshape(64, DH).astype(jnp.bfloat16)
        keys = kbuf[pl.ds(2 * p, 2)].reshape(2 * LEN, DH)
        values = vbuf[pl.ds(2 * p, 2)].reshape(2 * LEN, DH)
        token = lax.rem(lax.broadcasted_iota(jnp.int32, (64, 1), 0), 8)
        second = token >= STEPS
        low = jnp.where(second, LEN, 0)
        high = low + jnp.where(second, len_ref[2 * p + 1], len_ref[2 * p])
        slot = lax.broadcasted_iota(jnp.int32, (64, 2 * LEN), 1)
        old = lax.dot_general(queries, keys, contract_last, preferred_element_type=jnp.float32) * score_scale
        old = jnp.where((slot >= low) & (slot < high), old, -1e30)
        column = lax.broadcasted_iota(jnp.int32, (64, TOK), 1)
        last = p * 8 + token
        begin = p * 8 + jnp.where(second, STEPS, 0)
        new = lax.dot_general(queries, knew[...], contract_last, preferred_element_type=jnp.float32) * score_scale
        new = jnp.where((column >= begin) & (column <= last), new, -1e30)
        highest = jnp.maximum(jnp.max(old, -1, keepdims=True), jnp.max(new, -1, keepdims=True))
        old_exp = jnp.exp(old - highest)
        new_exp = jnp.exp(new - highest)
        inverse = 1.0 / (jnp.sum(old_exp, -1, keepdims=True) + jnp.sum(new_exp, -1, keepdims=True))
        old_weights = (old_exp * inverse).astype(jnp.bfloat16)
        new_weights = (new_exp * inverse).astype(jnp.bfloat16)
        mixture = jnp.dot(old_weights, values, preferred_element_type=jnp.float32)
        mixture = mixture + jnp.dot(new_weights, vnew[...], preferred_element_type=jnp.float32)
        for g in range(8):
            mixed[tokens, g * DH : (g + 1) * DH] = mixture[g * 8 : (g + 1) * 8]

    QT = TOK // 4

    def h_rows(qt):
        return heads.at[pl.ds(pl.multiple_of(qt * QT, QT), QT)]

    def h_slot(qt):
        return hbuf.at[xl, pl.ds(pl.multiple_of(qt * QT, QT), QT), pl.ds(pl.multiple_of(half * OUT, OUT), OUT)]

    def h_send(qt, d):
        return remote(h_rows(qt), h_slot(qt), h_ss.at[qt, d], h_rs.at[xl, half, qt], h_target(d))

    def h_local(qt):
        return pltpu.make_async_copy(h_rows(qt), h_slot(qt), h_rs.at[xl, half, qt])

    def quarter(qt, carry):
        for n in range(4):
            attend_pair(qt * 4 + n)
        rows = pl.ds(pl.multiple_of(qt * QT, QT), QT)
        heads[rows] = mixed[rows].astype(jnp.bfloat16)
        for d in (1, 3, 2):
            h_send(qt, d).start()

        @pl.when(here)
        def _():
            h_local(qt).start()

        @pl.when(jnp.logical_not(here))
        def _():
            h_send(qt, 0).start()

        return carry

    lax.fori_loop(0, 4, quarter, 0)

    for d in (0, 1, 3, 2):
        r2_wait(d)
        r3_copy(3, d).start()
    for source in range(4):
        for d in range(4):
            r3_wait(source, d)
    o_keep().wait()

    for i in range(2):
        for h in range(2):
            for qt in range(4):
                ref = hbuf.at[i, pl.ds(qt * QT, QT), pl.ds(h * OUT, OUT)]
                pltpu.make_async_copy(ref, ref, h_rs.at[i, h, qt]).wait()

    def mine(i, j):
        return (z_rows == z) & (xl == i) & (y == 2 * xl + j)

    def d_copy(n, j, i):
        return remote(
            dsend.at[j, n, i], drecv.at[n, z], d_ss.at[j, n, i], d_rs.at[n, z], d_target(i, j)
        )

    def d_local(n, j, i):
        return pltpu.make_async_copy(dsend.at[j, n, i], drecv.at[n, z], d_rs.at[n, z])

    for n in range(NO):
        for j in range(2):
            lo = j * OUT + n * CW
            w = wo_ref[:, :, lo : lo + CW].reshape(PLANE, CW)
            part = jnp.dot(hbuf[...].reshape(2 * TOK, PLANE), w, preferred_element_type=jnp.float32)
            dsend[j, n] = part.astype(jnp.bfloat16).reshape(2, TOK, CW)
            for i in range(2):

                @pl.when(mine(i, j))
                def _():
                    d_local(n, j, i).start()

                @pl.when(jnp.logical_not(mine(i, j)))
                def _():
                    d_copy(n, j, i).start()

    for n in range(NO):
        total = None
        for p in range(4):
            ref = drecv.at[n, p]
            pltpu.make_async_copy(ref, ref, d_rs.at[n, p]).wait()
            part = drecv[n, p].astype(jnp.float32)
            total = part if total is None else total + part
        out_ref[:, :, n * CW : (n + 1) * CW] = total.reshape(TOK // STEPS, STEPS, CW).astype(jnp.bfloat16)

    def drain_heads(qt, carry):
        for d in range(1, 4):
            h_send(qt, d).wait_send()

        @pl.when(jnp.logical_not(here))
        def _():
            h_send(qt, 0).wait_send()

        return carry

    lax.fori_loop(0, 4, drain_heads, 0)
    for n in range(NO):
        for j in range(2):
            for i in range(2):

                @pl.when(jnp.logical_not(mine(i, j)))
                def _():
                    d_copy(n, j, i).wait_send()

    for e in range(1, 4):
        a_copy(e).wait_send()

    def drain(ch, carry):
        for d in range(1, 8):
            w1_copy(ch, d).wait_send()
        for g in range(2):
            w2_copy(ch, g).wait_send()
        for g in range(4):
            w3_copy(ch, g).wait_send()
        for k in range(2):
            cx_copy(ch, k).wait_send()
            for n in range(2):
                c_copy(ch, n, k).wait_send()
        return carry

    lax.fori_loop(0, NC, drain, 0)
    for d in range(1, 4):
        o1_copy(d).wait_send()
    for d in range(4):
        r1_copy(0, d).wait_send()
        r1_copy(1, d).wait_send()
        r2_copy(d).wait_send()
        for source in range(4):
            r3_copy(source, d).wait_send()


VM = pl.BlockSpec(memory_space=pltpu.VMEM)
ANY = pl.BlockSpec(memory_space=pl.ANY)
DMA = pltpu.SemaphoreType.DMA


def run_layer(normed, joined, merged_output, cosine, sine, lengths, keys, values):
    return pl.pallas_call(
        layer_kernel,
        out_shape=jax.ShapeDtypeStruct((TOK // STEPS, STEPS, OUT), jnp.bfloat16),
        in_specs=[ANY, ANY, ANY, VM, VM, pl.BlockSpec(memory_space=pltpu.SMEM), ANY, ANY],
        out_specs=VM,
        scratch_shapes=[
            pltpu.VMEM((4, TOK, PLANE), jnp.bfloat16),
            pltpu.VMEM((NC, 32, WROWS, CW), jnp.bfloat16),
            pltpu.VMEM((NC, 4, 2, TOK, DH), jnp.float32),
            pltpu.VMEM((NC, 2, TOK, DH), jnp.float32),
            pltpu.VMEM((NC, 2, 2, TOK, DH), jnp.float32),
            pltpu.VMEM((WROWS, 2 * OUT), jnp.bfloat16),
            pltpu.VMEM((32, WROWS, 2 * OUT), jnp.bfloat16),
            pltpu.VMEM(keys.shape, jnp.bfloat16),
            pltpu.VMEM(values.shape, jnp.bfloat16),
            pltpu.VMEM((8, TOK, DH), jnp.float32),
            pltpu.VMEM((TOK, DH), jnp.bfloat16),
            pltpu.VMEM((TOK, DH), jnp.bfloat16),
            pltpu.VMEM((TOK, OUT), jnp.float32),
            pltpu.VMEM((TOK, OUT), jnp.bfloat16),
            pltpu.VMEM((2, TOK, PLANE), jnp.bfloat16),
            pltpu.VMEM((2, NO, 2, TOK, CW), jnp.bfloat16),
            pltpu.VMEM((NO, 4, TOK, CW), jnp.bfloat16),
            DMA((4,)), DMA((4,)),
            DMA((NC, 8)), DMA((NC, 8)),
            DMA((NC, 2)), DMA((NC, 2)),
            DMA((NC, 4)), DMA((NC, 4)),
            DMA((NC, 2)), DMA((NC, 2)),
            DMA((NC, 2, 2)), DMA((NC, 2, 2)),
            DMA((4,)), DMA((4,)),
            DMA((2, 4)), DMA((2, 4)),
            DMA((4,)), DMA((4,)),
            DMA((4, 4)), DMA((4, 4)),
            DMA((2,)),
            DMA((4, 4)), DMA((2, 2, 4)),
            DMA((2, NO, 2)), DMA((NO, 4)),
        ],
        compiler_params=pltpu.CompilerParams(collective_id=0, has_side_effects=True, vmem_limit_bytes=62 << 20),
        name="layer",
    )(normed, joined, merged_output, cosine, sine, lengths, keys, values)


def prepare_kernel(
    slot_ref, gain_ref, states_ref, q_ref, k_ref, v_ref, o_ref,
    qd_ref, kd_ref, vd_ref, od_ref, qu_ref, ku_ref, vu_ref, ou_ref,
    normed_ref, joined_ref, merged_ref,
):
    def merge(base, down, up):
        delta = jnp.dot(down[0], up[0], preferred_element_type=jnp.float32)
        return (base[...].astype(jnp.float32) + low_rank_scale * delta).astype(jnp.bfloat16)

    q, k, v = merge(q_ref, qd_ref, qu_ref), merge(k_ref, kd_ref, ku_ref), merge(v_ref, vd_ref, vu_ref)
    for n in range(joined_ref.shape[1] // QKV):
        base = n * QKV
        joined_ref[:, base : base + OUT] = q[:, n * OUT : (n + 1) * OUT]
        joined_ref[:, base + OUT : base + OUT + DH] = k[:, n * DH : (n + 1) * DH]
        joined_ref[:, base + OUT + DH : base + QKV] = v[:, n * DH : (n + 1) * DH]
    merged_ref[...] = merge(o_ref, od_ref, ou_ref)
    widened = states_ref[...].astype(jnp.float32)
    squared_average = jnp.mean(widened * widened, axis=-1, keepdims=True)
    normed = widened * lax.rsqrt(squared_average + epsilon) * gain_ref[...].reshape(1, 1, -1)
    normed_ref[...] = normed.reshape(normed_ref.shape).astype(jnp.bfloat16)


def prepare(slot, gain, states, bases, downs, ups):
    steps = 2
    seqs, decode, width = states.shape
    block = seqs // steps

    def cols(array):
        return pl.BlockSpec((array.shape[0], array.shape[1] // steps), lambda i, s: (0, i))

    def down(array):
        return pl.BlockSpec((1, *array.shape[1:]), lambda i, s: (s[0], 0, 0))

    def up(array):
        return pl.BlockSpec((1, array.shape[1], array.shape[2] // steps), lambda i, s: (s[0], 0, i))

    return pl.pallas_call(
        prepare_kernel,
        out_shape=(
            jax.ShapeDtypeStruct((seqs * decode, width), jnp.bfloat16),
            jax.ShapeDtypeStruct((WROWS, QKV * 8), jnp.bfloat16),
            jax.ShapeDtypeStruct((WROWS, OUT * 8), jnp.bfloat16),
        ),
        grid_spec=pltpu.PrefetchScalarGridSpec(
            num_scalar_prefetch=1,
            grid=(steps,),
            in_specs=[
                pl.BlockSpec((1, width), lambda i, s: (0, 0)),
                pl.BlockSpec((block, decode, width), lambda i, s: (i, 0, 0)),
                *[cols(b) for b in bases],
                *[down(d) for d in downs],
                *[up(u) for u in ups],
            ],
            out_specs=(
                pl.BlockSpec((block * decode, width), lambda i, s: (i, 0)),
                pl.BlockSpec((WROWS, QKV * 8 // steps), lambda i, s: (0, i)),
                pl.BlockSpec((WROWS, OUT * 8 // steps), lambda i, s: (0, i)),
            ),
        ),
        name="prepare",
    )(slot, gain.reshape(1, -1), states, *bases, *downs, *ups)


def rope_tables(positions):
    half_dim = DH // 2
    frequency = rope_theta ** (-2.0 * jnp.arange(half_dim, dtype=jnp.float32) / DH)
    rotation_phases = positions[:, None] * frequency[None, :]
    cosine, sine = jnp.cos(rotation_phases), jnp.sin(rotation_phases)
    return jnp.concatenate((cosine, cosine), -1), jnp.concatenate((-sine, sine), -1)


def local(
    states,
    norm_gain,
    query_base,
    key_base,
    value_base,
    output_base,
    query_down,
    query_up,
    key_down,
    key_up,
    value_down,
    value_up,
    output_down,
    output_up,
    adapter_layer,
    kv_lengths,
    cache_keys,
    cache_values,
):
    seq_count, step_count, _ = states.shape
    normed, joined, merged_output = prepare(
        adapter_layer,
        norm_gain,
        states,
        (query_base, key_base, value_base, output_base),
        (query_down, key_down, value_down, output_down),
        (query_up, key_up, value_up, output_up),
    )
    positions = (
        kv_lengths.astype(jnp.float32)[:, None] + jnp.arange(step_count, dtype=jnp.float32)[None, :]
    )
    cosine, sine = rope_tables(positions.reshape(-1))
    keys = cache_keys.reshape(seq_count, -1, DH)
    values = cache_values.reshape(seq_count, -1, DH)
    return run_layer(normed, joined, merged_output, cosine, sine, kv_lengths, keys, values)


def solution(mesh):
    in_specs = (
        P("fsdp", None, None),
        P(),
        P(("fsdp", "tp"), None),
        P(("fsdp", "tp"), None),
        P(("fsdp", "tp"), None),
        P(("fsdp", "tp"), None),
        P(None, ("fsdp", "tp"), None),
        P(),
        P(None, ("fsdp", "tp"), None),
        P(),
        P(None, ("fsdp", "tp"), None),
        P(),
        P(None, ("fsdp", "tp"), None),
        P(),
        P(),
        P("fsdp"),
        P("fsdp", None, "tp", None),
        P("fsdp", None, "tp", None),
    )
    out_specs = P("fsdp", None, "tp")
    return jax.shard_map(local, mesh=mesh, in_specs=in_specs, out_specs=out_specs, check_vma=False)
```
